128 devices in a mesh: song: 2 (over y_lo), seq: 64 (over z, x, y_hi, core).
Axes of the slice: x: 4, y: 4 (y_hi: 2, y_lo: 2; y = y_hi * 2 + y_lo), z: 4, core: 2. Of those that a mesh axis runs over, the one named last changes fastest.
Arguments:
- song_ids: int32 [16384], P(('song', 'seq')), parts along dimension 0, may hold values from 0 to 2047
- table: bfloat16 [2048, 2432], P(None, 'seq'), may hold values from -6 to 6
- position_table: bfloat16 [8192, 2432], P('seq'), may hold values from -4 to 4
- w_qkv: bfloat16 [2, 2432, 1800], replicated, may hold values from -4 to 4
- w_out: bfloat16 [2, 600, 2432], replicated, may hold values from -0.25 to 0.25
Outputs:
- stream_out: bfloat16 [16384, 2432], P(('song', 'seq')), parts along dimension 0
The draws below stay inside these ranges and needn't reach their ends.
There are 2 independent parts, one for each index of `song`. The reference program is written for one: setup_inputs(seed, part) draws one part's arguments, and reference() takes and returns one part's arrays. A program takes and returns all parts, laid end to end along the dimension named above; an argument that names none is the same for every part. Nothing has to cross between parts.
All inputs are finite; a program needn't handle non-finite values.
Results may differ from the reference program's by a relative error of at most 0.0065.
Values may be sent and summed in bfloat16 or wider, within the bound.
No kernel may reach another device: no remote copies, remote signals or barrier semaphores. Data moves between devices by JAX's collectives and lax.ppermute only.
A program may use at most 192 MiB of HBM per device.

```python
import math
import jax
import jax.numpy as jnp
import numpy as np
from jax import lax

D = 2432
HEADS = 4
HEAD = 150
VOCAB = 2048
ROW_TOKENS = 128
LAYERS = 2
ATT = 600
ROWS = 64
TOKENS = 8192


def draw_w_qkv(key, part):
    spread = D ** (-0.5)
    base = jax.random.normal(key, (LAYERS, D, 3 * ATT), jnp.float32) * spread
    base = jnp.clip(base, -6.0 * spread, 6.0 * spread)
    return jnp.clip(base, -4.0, 4.0).astype(jnp.bfloat16)


def plant(drawn, key, low, top_value):
    longest = drawn.shape.index(max(drawn.shape))
    spots = []
    for shift in (0, 1):
        where = [jax.random.randint(jax.random.fold_in(key, axis), (), 0, length) for axis, length in enumerate(drawn.shape)]
        where[longest] = (where[longest] + shift) % drawn.shape[longest]
        spots.append(tuple(where))
    return drawn.at[spots[0]].set(low).at[spots[1]].set(top_value)


def shard_levels(own_key, extent, shards, smallest, top_value):
    gain, own = 1.0, jax.random.fold_in(own_key, 6)
    for position, parts in shards:
        steps = jnp.exp(jax.random.uniform(jax.random.fold_in(own, position), (parts,), jnp.float32, smallest / len(shards), top_value / len(shards)))
        gain = gain * jnp.repeat(steps, extent[position] // parts).reshape([-1 if axis == position else 1 for axis in range(len(extent))])
    return gain


def rank_bounds(amount, slope):
    weights = [(1 << 20) // math.isqrt(rank ** slope) + 1 for rank in range(1, amount + 1)]
    scale = 1 + sum(weights) // (1 << 30)
    return np.cumsum(np.array([max(1, weight // scale) for weight in weights]))


def ranked_ids(key, dims, number_of, skew):
    table = rank_bounds(number_of, skew)
    pick = jax.random.randint(jax.random.fold_in(key, 1), dims, 0, int(table[number_of - 1]))
    standing = jnp.searchsorted(jnp.asarray(table, jnp.int32), pick, side="right")
    return jax.random.permutation(jax.random.fold_in(key, 2), number_of)[standing].astype(jnp.int32)


def noise(rng, dims, width, most, cuts=(), held_as=jnp.bfloat16):
    values = jax.random.normal(rng, dims, jnp.float32) * width
    if len(cuts) > 0:
        values = shard_levels(rng, dims, cuts, -0.22, 0.18) * values
    return jnp.clip(values, min=-most, max=most).astype(held_as)


def setup_inputs(seed: int = 0, part: int = 0) -> dict:
    seeds = jax.random.split(jax.random.key(seed), 6)
    part_keys = jax.random.split(jax.random.fold_in(seeds[5], part), 6)
    song_ids = plant(ranked_ids(part_keys[0], (TOKENS,), VOCAB, 2), jax.random.fold_in(part_keys[0], 3), 0, VOCAB - 1).astype(jnp.int32)
    table = noise(seeds[1], (VOCAB, D), 1.0, 6.0, ((1, 64),))
    position_table = noise(seeds[2], (TOKENS, D), 0.5, 4.0, ((0, 64),))
    w_qkv = draw_w_qkv(jax.random.fold_in(seeds[5], 71), part)
    w_out = noise(seeds[4], (LAYERS, ATT, D), ATT ** -0.5, 0.25)
    return {"song_ids": song_ids, "table": table, "position_table": position_table, "w_qkv": w_qkv, "w_out": w_out}


epsilon = 1e-05

def normalize(residual):
    center_mean = lax.optimization_barrier(jnp.mean(residual, axis=-1, keepdims=True))
    centered = residual - center_mean
    variance = lax.optimization_barrier(jnp.mean(centered * centered, axis=-1, keepdims=True))
    return (centered * lax.rsqrt(variance + epsilon)).astype(jnp.bfloat16)

def project(residual, weight):
    joined = jnp.dot(normalize(residual), weight, preferred_element_type=jnp.float32).astype(jnp.bfloat16)
    return joined.reshape(ROWS, ROW_TOKENS, HEADS, 3 * HEAD).astype(jnp.float32)

def reference(song_ids, table, position_table, w_qkv, w_out):
    inv_root = 1.0 / math.sqrt(HEAD)
    residual = table[song_ids].astype(jnp.float32) + position_table.astype(jnp.float32)
    row_ids = jnp.arange(ROWS)
    joined = project(residual, w_qkv[0])
    query = joined[..., :HEAD]
    keys_col = joined[..., HEAD:2 * HEAD]
    values_col = joined[..., 2 * HEAD:]
    scores = jnp.einsum('rchd,schd->chrs', query, keys_col) * inv_root
    allowed = row_ids[None, :] <= row_ids[:, None]
    scores = jnp.where(allowed, scores, -jnp.inf)
    top_score = lax.optimization_barrier(jnp.max(scores, axis=-1, keepdims=True))
    lifted = jnp.exp(scores - top_score)
    probs = (lifted / lax.optimization_barrier(jnp.sum(lifted, axis=-1, keepdims=True))).astype(jnp.bfloat16).astype(jnp.float32)
    mixed = jnp.einsum('chrs,schd->rchd', probs, values_col).astype(jnp.bfloat16).reshape(TOKENS, ATT)
    residual = residual + jnp.dot(mixed, w_out[0], preferred_element_type=jnp.float32)
    joined = project(residual, w_qkv[1])
    query = joined[..., :HEAD]
    keys_row = joined[..., HEAD:2 * HEAD]
    values_row = joined[..., 2 * HEAD:]
    keys_prev = jnp.concatenate([jnp.zeros_like(keys_row[:1]), keys_row[:-1]], axis=0)
    values_prev = jnp.concatenate([jnp.zeros_like(values_row[:1]), values_row[:-1]], axis=0)
    far_scores = jnp.einsum('rchd,rkhd->rhck', query, keys_prev) * inv_root
    far_scores = jnp.where((row_ids > 0)[:, None, None, None], far_scores, -jnp.inf)
    own_scores = jnp.einsum('rchd,rchd->rhc', query, keys_row)[..., None] * inv_root
    scores = jnp.concatenate([far_scores, own_scores], axis=-1)
    top_score = lax.optimization_barrier(jnp.max(scores, axis=-1, keepdims=True))
    lifted = jnp.exp(scores - top_score)
    probs = (lifted / lax.optimization_barrier(jnp.sum(lifted, axis=-1, keepdims=True))).astype(jnp.bfloat16).astype(jnp.float32)
    far_part = jnp.einsum('rhck,rkhd->rchd', probs[..., :-1], values_prev)
    own_part = jnp.transpose(probs[..., -1], (0, 2, 1))[..., None] * values_row
    mixed = (far_part + own_part).astype(jnp.bfloat16).reshape(TOKENS, ATT)
    residual = residual + jnp.dot(mixed, w_out[1], preferred_element_type=jnp.float32)
    return residual.astype(jnp.bfloat16)
```

```python
import functools
import math

import jax
import jax.numpy as jnp
from jax import lax
from jax.experimental import pallas as pl
from jax.experimental.pallas import tpu as pltpu
from jax.sharding import PartitionSpec as P

HEADS = 4
HEAD = 150
GROUPS = 8

epsilon = 1e-05


def normalize(residual):
    center_mean = jnp.mean(residual, axis=-1, keepdims=True)
    centered = residual - center_mean
    variance = jnp.mean(centered * centered, axis=-1, keepdims=True)
    return (centered * lax.rsqrt(variance + epsilon)).astype(jnp.bfloat16)


def project(residual, weight):
    return jnp.dot(normalize(residual), weight, preferred_element_type=jnp.float32).astype(
        jnp.bfloat16
    )


def lookup_kernel(codes_ref, table_ref, out_ref):
    depth = table_ref.shape[1]
    step = table_ref.shape[0] // GROUPS
    count = out_ref.shape[0]
    table_rows = table_ref[...].astype(jnp.float32)
    padded = (depth + 7) // 8 * 8
    flipped = jnp.transpose(
        jnp.concatenate(
            [table_rows, jnp.zeros((table_rows.shape[0], 128 - depth), jnp.float32)], axis=1
        )
    )[:padded]
    stacked = jnp.concatenate(
        [flipped[:, g * step : (g + 1) * step] for g in range(GROUPS)], axis=0
    ).astype(jnp.bfloat16)
    slots = lax.broadcasted_iota(jnp.int32, (step, 128), 0)
    for d in range(count):
        codes = codes_ref[d : d + 1, :]
        low = codes % step
        high = codes // step
        onehot = jnp.where(slots == low, 1.0, 0.0).astype(jnp.bfloat16)
        found = jnp.dot(stacked, onehot, preferred_element_type=jnp.float32)
        chosen = jnp.zeros((padded, 128), jnp.float32)
        for g in range(GROUPS):
            chosen = jnp.where(high == g, found[g * padded : (g + 1) * padded], chosen)
        out_ref[d] = chosen[:depth].astype(jnp.bfloat16)


def lookup(codes, table):
    count = codes.shape[0]
    depth = table.shape[1]
    return pl.pallas_call(
        lookup_kernel,
        out_shape=jax.ShapeDtypeStruct((count, depth, 128), jnp.bfloat16),
        in_specs=[pl.BlockSpec(memory_space=pltpu.VMEM)] * 2,
        out_specs=pl.BlockSpec(memory_space=pltpu.VMEM),
        compiler_params=pltpu.CompilerParams(vmem_limit_bytes=16 * 1024 * 1024),
    )(codes, table)


def exchange(value):
    return lax.all_to_all(value, "seq", split_axis=0, concat_axis=0, tiled=True)


def shards(song_ids, table, position_table, w_qkv, w_out):
    inv_root = 1.0 / math.sqrt(HEAD)
    rows = lax.axis_size("seq")
    row_index = lax.axis_index("seq")
    tokens, width = position_table.shape
    per = tokens // rows
    attended = HEADS * HEAD

    digits = jnp.stack([song_ids // 64, song_ids % 64]).astype(jnp.bfloat16)
    sent = jnp.concatenate(
        [
            position_table.reshape(rows, per, width),
            jnp.broadcast_to(digits[None], (rows, 2, tokens)),
        ],
        axis=-1,
    )
    got = exchange(sent)
    position = got[:, :, :width].reshape(tokens, width)
    codes = got[:, 0, width:].astype(jnp.int32) * 64 + got[:, 1, width:].astype(jnp.int32)
    codes = jnp.transpose(codes.reshape(rows, rows, per), (1, 2, 0)).reshape(rows, tokens)
    found = exchange(lookup(codes, table))
    embedded = jnp.transpose(found.reshape(rows, -1, per, rows), (3, 2, 0, 1)).reshape(
        tokens, width
    )
    residual = embedded.astype(jnp.float32) + position.astype(jnp.float32)

    joined = project(residual, w_qkv[0]).reshape(tokens, HEADS, 3 * HEAD)
    scores = (
        jnp.einsum(
            "thd,uhd->htu",
            joined[:, :, :HEAD],
            joined[:, :, HEAD : 2 * HEAD],
            preferred_element_type=jnp.float32,
        )
        * inv_root
    )
    place = jnp.arange(tokens)
    allowed = (place[:, None] % per == place[None, :] % per) & (place[:, None] >= place[None, :])
    scores = jnp.where(allowed, scores, -jnp.inf)
    lifted = jnp.exp(scores - jnp.max(scores, axis=-1, keepdims=True))
    probs = (lifted / jnp.sum(lifted, axis=-1, keepdims=True)).astype(jnp.bfloat16)
    mixed = jnp.einsum(
        "htu,uhd->thd", probs, joined[:, :, 2 * HEAD :], preferred_element_type=jnp.float32
    ).astype(jnp.bfloat16)
    residual = residual + jnp.dot(
        mixed.reshape(tokens, attended), w_out[0], preferred_element_type=jnp.float32
    )

    residual = exchange(residual.astype(jnp.bfloat16).reshape(rows, per, width))
    residual = residual.reshape(tokens, width).astype(jnp.float32)
    joined = project(residual, w_qkv[1]).reshape(tokens, HEADS, 3 * HEAD)
    before = lax.ppermute(
        joined[:, :, HEAD:], "seq", [(i, i + 1) for i in range(rows - 1)]
    )
    query = joined[:, :, :HEAD]
    far_scores = (
        jnp.einsum("chd,khd->hck", query, before[..., :HEAD], preferred_element_type=jnp.float32)
        * inv_root
    )
    far_scores = jnp.where(row_index > 0, far_scores, -jnp.inf)
    own_scores = (
        jnp.einsum(
            "chd,chd->hc", query, joined[:, :, HEAD : 2 * HEAD], preferred_element_type=jnp.float32
        )
        * inv_root
    )
    top_score = jnp.maximum(jnp.max(far_scores, axis=-1), own_scores)
    far_lifted = jnp.exp(far_scores - top_score[..., None])
    own_lifted = jnp.exp(own_scores - top_score)
    total = jnp.sum(far_lifted, axis=-1) + own_lifted
    far_probs = (far_lifted / total[..., None]).astype(jnp.bfloat16)
    own_probs = (own_lifted / total).astype(jnp.bfloat16)
    far_part = jnp.einsum(
        "hck,khd->chd", far_probs, before[..., HEAD:], preferred_element_type=jnp.float32
    )
    own_part = jnp.transpose(own_probs.astype(jnp.float32))[..., None] * joined[
        :, :, 2 * HEAD :
    ].astype(jnp.float32)
    mixed = (far_part + own_part).astype(jnp.bfloat16)
    residual = residual + jnp.dot(
        mixed.reshape(tokens, attended), w_out[1], preferred_element_type=jnp.float32
    )
    return residual.astype(jnp.bfloat16)


def solution(mesh):
    in_specs = (P(("song", "seq")), P(None, "seq"), P("seq", None), P(), P())
    out_specs = P(("song", "seq"), None)
    return jax.shard_map(shards, mesh=mesh, in_specs=in_specs, out_specs=out_specs, check_vma=False)
```

```python
import functools
import math

import jax
import jax.numpy as jnp
from jax import lax
from jax.experimental import pallas as pl
from jax.experimental.pallas import tpu as pltpu
from jax.sharding import PartitionSpec as P

HEADS = 4
HEAD = 150
GROUPS = 8
DIGIT = 64
STRIPS = 4
VMEM_LIMIT = 32 * 1024 * 1024
WEIGHTS = pltpu.HBM

epsilon = 1e-05


def normalize(x_ref, normed_ref):
    width = x_ref.shape[1]
    blocks = [slice(i, min(i + 128, width)) for i in range(0, width, 128)]
    total = sum(x_ref[:, b] for b in blocks)
    mean = jnp.sum(total, axis=1, keepdims=True) * (1.0 / width)
    total = jnp.zeros_like(total)
    for b in blocks:
        centered = x_ref[:, b] - mean
        total += centered * centered
    scale = lax.rsqrt(jnp.sum(total, axis=1, keepdims=True) * (1.0 / width) + epsilon)
    for b in blocks:
        normed_ref[:, b] = ((x_ref[:, b] - mean) * scale).astype(jnp.bfloat16)


def strips(count):
    step = -(-count // (STRIPS * 128)) * 128
    return [(i, min(i + step, count)) for i in range(0, count, step)]


def fetches(layer, w_in_hbm, w_out_hbm, w_in_ref, w_out_ref, sem):
    parts = strips(w_in_hbm.shape[1])
    copies = [
        pltpu.make_async_copy(w_in_hbm.at[layer, lo:hi], w_in_ref.at[lo:hi], sem.at[i])
        for i, (lo, hi) in enumerate(parts)
    ]
    if w_out_hbm is not None:
        copies.append(pltpu.make_async_copy(w_out_hbm.at[layer], w_out_ref, sem.at[len(parts)]))
    return copies


def project_strips(normed_ref, w_in_ref, joined_ref, copies):
    for (lo, hi), copy in zip(strips(w_in_ref.shape[0]), copies):
        copy.wait()
        joined_ref[:, lo:hi] = lax.dot_general(
            normed_ref[...],
            w_in_ref[lo:hi],
            (((1,), (1,)), ((), ())),
            preferred_element_type=jnp.float32,
        ).astype(jnp.bfloat16)


def column_kernel(
    found_ref, got_ref, w_in_hbm, w_out_hbm, out_ref,
    flat_ref, x_ref, normed_ref, joined_ref, w_in_ref, w_out_ref, sem,
):
    rows, depth, tokens = found_ref.shape
    per = out_ref.shape[1]
    width = out_ref.shape[2]
    copies = fetches(0, w_in_hbm, w_out_hbm, w_in_ref, w_out_ref, sem)
    for copy in copies:
        copy.start()
    for s in range(rows):
        flat_ref[s * depth : (s + 1) * depth] = found_ref[s].astype(jnp.float32)
    for r in range(rows):
        x_ref[r * per : (r + 1) * per] = got_ref[r, :, :width].astype(jnp.float32)
    for i in range(0, width, 128):
        x_ref[:, i : i + 128] += jnp.transpose(flat_ref[i : i + 128])
    normalize(x_ref, normed_ref)
    project_strips(normed_ref, w_in_ref, joined_ref, copies)
    joined = joined_ref[...]
    row_of = lax.broadcasted_iota(jnp.int32, (tokens, tokens), 0)
    col_of = lax.broadcasted_iota(jnp.int32, (tokens, tokens), 1)
    allowed = (row_of % per == col_of % per) & (row_of >= col_of)
    pieces = []
    for h in range(HEADS):
        base = 3 * HEAD * h
        query = joined[:, base : base + HEAD]
        key = joined[:, base + HEAD : base + 2 * HEAD]
        value = joined[:, base + 2 * HEAD : base + 3 * HEAD]
        scores = lax.dot_general(
            query, key, (((1,), (1,)), ((), ())), preferred_element_type=jnp.float32
        ) * (1.0 / math.sqrt(HEAD))
        scores = jnp.where(allowed, scores, -jnp.inf)
        lifted = jnp.exp(scores - jnp.max(scores, axis=1, keepdims=True))
        probs = (lifted / jnp.sum(lifted, axis=1, keepdims=True)).astype(jnp.bfloat16)
        pieces.append(
            jnp.dot(probs, value, preferred_element_type=jnp.float32).astype(jnp.bfloat16)
        )
    mixed = jnp.concatenate(pieces, axis=1)
    copies[-1].wait()
    normed_ref[...] = (
        x_ref[...] + jnp.dot(mixed, w_out_ref[...], preferred_element_type=jnp.float32)
    ).astype(jnp.bfloat16)
    for r in range(rows):
        out_ref[r] = normed_ref[r * per : (r + 1) * per]


def column_sublayer(found, got, w_in, w_out):
    rows, depth, tokens = found.shape
    joint, width = w_in.shape[1:]
    per = tokens // rows
    return pl.pallas_call(
        column_kernel,
        out_shape=jax.ShapeDtypeStruct((rows, per, width), jnp.bfloat16),
        in_specs=[pl.BlockSpec(memory_space=pltpu.VMEM)] * 2
        + [pl.BlockSpec(memory_space=WEIGHTS)] * 2,
        out_specs=pl.BlockSpec(memory_space=pltpu.VMEM),
        scratch_shapes=[
            pltpu.VMEM((width, tokens), jnp.float32),
            pltpu.VMEM((tokens, width), jnp.float32),
            pltpu.VMEM((tokens, width), jnp.bfloat16),
            pltpu.VMEM((tokens, joint), jnp.bfloat16),
            pltpu.VMEM((joint, width), jnp.bfloat16),
            pltpu.VMEM(w_out.shape[1:], jnp.bfloat16),
            pltpu.SemaphoreType.DMA((STRIPS + 1,)),
        ],
        compiler_params=pltpu.CompilerParams(vmem_limit_bytes=VMEM_LIMIT),
    )(found, got, w_in, w_out)


def project_kernel(resid_ref, w_in_hbm, own_ref, sent_ref, x_ref, normed_ref, w_in_ref, sem):
    rows, per, width = resid_ref.shape
    copies = fetches(1, w_in_hbm, None, w_in_ref, None, sem)
    for copy in copies:
        copy.start()
    for r in range(rows):
        x_ref[r * per : (r + 1) * per] = resid_ref[r].astype(jnp.float32)
    normalize(x_ref, normed_ref)
    project_strips(normed_ref, w_in_ref, own_ref, copies)
    joined = own_ref[...]
    sent_ref[...] = jnp.concatenate(
        [joined[:, 3 * HEAD * h + HEAD : 3 * HEAD * (h + 1)] for h in range(HEADS)], axis=1
    )


def project(resid, w_in):
    rows, per, width = resid.shape
    tokens = rows * per
    return pl.pallas_call(
        project_kernel,
        out_shape=(
            jax.ShapeDtypeStruct((tokens, 3 * HEADS * HEAD), jnp.bfloat16),
            jax.ShapeDtypeStruct((tokens, 2 * HEADS * HEAD), jnp.bfloat16),
            jax.ShapeDtypeStruct((tokens, width), jnp.float32),
        ),
        in_specs=[pl.BlockSpec(memory_space=pltpu.VMEM), pl.BlockSpec(memory_space=WEIGHTS)],
        out_specs=(pl.BlockSpec(memory_space=pltpu.VMEM),) * 3,
        scratch_shapes=[
            pltpu.VMEM((tokens, width), jnp.bfloat16),
            pltpu.VMEM(w_in.shape[1:], jnp.bfloat16),
            pltpu.SemaphoreType.DMA((STRIPS,)),
        ],
        compiler_params=pltpu.CompilerParams(vmem_limit_bytes=VMEM_LIMIT),
    )(resid, w_in)


def row_kernel(own_ref, before_ref, x_ref, w_out_hbm, out_ref, w_out_ref, sem):
    has_before = lax.axis_index("seq") > 0
    copy = pltpu.make_async_copy(w_out_hbm.at[1], w_out_ref, sem)
    copy.start()
    inv_root = 1.0 / math.sqrt(HEAD)
    joined = own_ref[...]
    before = before_ref[...]
    pieces = []
    for h in range(HEADS):
        base = 3 * HEAD * h
        query = joined[:, base : base + HEAD]
        key = joined[:, base + HEAD : base + 2 * HEAD].astype(jnp.float32)
        value = joined[:, base + 2 * HEAD : base + 3 * HEAD].astype(jnp.float32)
        far_key = before[:, 2 * HEAD * h : 2 * HEAD * h + HEAD]
        far_value = before[:, 2 * HEAD * h + HEAD : 2 * HEAD * (h + 1)]
        far_scores = (
            lax.dot_general(
                query, far_key, (((1,), (1,)), ((), ())), preferred_element_type=jnp.float32
            )
            * inv_root
        )
        far_scores = jnp.where(has_before, far_scores, -jnp.inf)
        own_scores = jnp.sum(query.astype(jnp.float32) * key, axis=1, keepdims=True) * inv_root
        top_score = jnp.maximum(jnp.max(far_scores, axis=1, keepdims=True), own_scores)
        far_lifted = jnp.exp(far_scores - top_score)
        own_lifted = jnp.exp(own_scores - top_score)
        total = jnp.sum(far_lifted, axis=1, keepdims=True) + own_lifted
        far_probs = (far_lifted / total).astype(jnp.bfloat16)
        own_probs = (own_lifted / total).astype(jnp.bfloat16).astype(jnp.float32)
        far_part = jnp.dot(far_probs, far_value, preferred_element_type=jnp.float32)
        pieces.append((far_part + own_probs * value).astype(jnp.bfloat16))
    mixed = jnp.concatenate(pieces, axis=1)
    copy.wait()
    out_ref[...] = (
        x_ref[...] + jnp.dot(mixed, w_out_ref[...], preferred_element_type=jnp.float32)
    ).astype(jnp.bfloat16)


def row_sublayer(own, before, x, w_out):
    return pl.pallas_call(
        row_kernel,
        out_shape=jax.ShapeDtypeStruct(x.shape, jnp.bfloat16),
        in_specs=[pl.BlockSpec(memory_space=pltpu.VMEM)] * 3
        + [pl.BlockSpec(memory_space=WEIGHTS)],
        out_specs=pl.BlockSpec(memory_space=pltpu.VMEM),
        scratch_shapes=[
            pltpu.VMEM(w_out.shape[1:], jnp.bfloat16),
            pltpu.SemaphoreType.DMA(()),
        ],
        compiler_params=pltpu.CompilerParams(vmem_limit_bytes=VMEM_LIMIT),
    )(own, before, x, w_out)


def lookup_kernel(codes_ref, table_ref, out_ref):
    depth, entries = table_ref.shape
    step = entries // GROUPS
    count = out_ref.shape[0]
    padded = (depth + 7) // 8 * 8
    flipped = jnp.concatenate(
        [table_ref[...].astype(jnp.float32), jnp.zeros((padded - depth, entries), jnp.float32)],
        axis=0,
    )
    stacked = jnp.concatenate(
        [flipped[:, g * step : (g + 1) * step] for g in range(GROUPS)], axis=0
    ).astype(jnp.bfloat16)
    slots = lax.broadcasted_iota(jnp.int32, (step, 128), 0)
    for d in range(count):
        codes = codes_ref[d : d + 1, :]
        low = codes % step
        high = codes // step
        onehot = jnp.where(slots == low, 1.0, 0.0).astype(jnp.bfloat16)
        found = jnp.dot(stacked, onehot, preferred_element_type=jnp.float32)
        chosen = jnp.zeros((padded, 128), jnp.float32)
        for g in range(GROUPS):
            chosen = jnp.where(high == g, found[g * padded : (g + 1) * padded], chosen)
        out_ref[d] = chosen[:depth].astype(jnp.bfloat16)


def lookup(codes, table):
    count = codes.shape[0]
    depth = table.shape[0]
    return pl.pallas_call(
        lookup_kernel,
        out_shape=jax.ShapeDtypeStruct((count, depth, 128), jnp.bfloat16),
        in_specs=[pl.BlockSpec(memory_space=pltpu.VMEM)] * 2,
        out_specs=pl.BlockSpec(memory_space=pltpu.VMEM),
        compiler_params=pltpu.CompilerParams(vmem_limit_bytes=16 * 1024 * 1024),
    )(codes, table)


def pack_kernel(codes_ref, position_ref, out_ref):
    rows, per, _ = out_ref.shape
    width = position_ref.shape[1]
    codes = codes_ref[...]
    digits = jnp.concatenate([codes // DIGIT, codes % DIGIT], axis=0).astype(jnp.bfloat16)
    for r in range(rows):
        out_ref[r, :, :width] = position_ref[r * per : (r + 1) * per]
        out_ref[r, :, width:] = digits


def pack(song_ids, position_table, rows):
    tokens, width = position_table.shape
    return pl.pallas_call(
        pack_kernel,
        out_shape=jax.ShapeDtypeStruct((rows, tokens // rows, width + tokens), jnp.bfloat16),
        in_specs=[pl.BlockSpec(memory_space=pltpu.VMEM)] * 2,
        out_specs=pl.BlockSpec(memory_space=pltpu.VMEM),
        compiler_params=pltpu.CompilerParams(vmem_limit_bytes=VMEM_LIMIT),
    )(song_ids.reshape(1, tokens), position_table)


def exchange(value):
    return lax.all_to_all(value, "seq", split_axis=0, concat_axis=0, tiled=True)


def shards(song_ids, table, position_table, w_qkv, w_out):
    rows = lax.axis_size("seq")
    tokens, width = position_table.shape
    per = tokens // rows

    got = exchange(pack(song_ids, position_table, rows))
    codes = got[:, 0, width:].astype(jnp.int32) * DIGIT + got[:, 1, width:].astype(jnp.int32)
    codes = jnp.transpose(codes.reshape(rows, rows, per), (1, 0, 2)).reshape(rows, tokens)
    found = exchange(lookup(codes, jnp.transpose(table)))
    w_in = jnp.swapaxes(w_qkv, 1, 2)
    resid = exchange(column_sublayer(found, got, w_in, w_out))
    own, sent, x = project(resid, w_in)
    before = lax.ppermute(sent, "seq", [(i, i + 1) for i in range(rows - 1)])
    return row_sublayer(own, before, x, w_out)


def solution(mesh):
    in_specs = (P(("song", "seq")), P(None, "seq"), P("seq", None), P(), P())
    out_specs = P(("song", "seq"), None)
    return jax.shard_map(shards, mesh=mesh, in_specs=in_specs, out_specs=out_specs, check_vma=False)
```

```python
import functools
import math

import jax
import jax.numpy as jnp
from jax import lax
from jax.experimental import pallas as pl
from jax.experimental.pallas import tpu as pltpu
from jax.sharding import PartitionSpec as P

HEADS = 4
HEAD = 150
GROUPS = 8
DIGIT = 64
VMEM_LIMIT = 12 * 1024 * 1024

epsilon = 1e-05


def normalize(x_ref, normed_ref):
    width = x_ref.shape[1]
    blocks = [slice(i, min(i + 128, width)) for i in range(0, width, 128)]
    total = sum(x_ref[:, b] for b in blocks)
    mean = jnp.sum(total, axis=1, keepdims=True) * (1.0 / width)
    total = jnp.zeros_like(total)
    for b in blocks:
        centered = x_ref[:, b] - mean
        total += centered * centered
    scale = lax.rsqrt(jnp.sum(total, axis=1, keepdims=True) * (1.0 / width) + epsilon)
    for b in blocks:
        normed_ref[:, b] = ((x_ref[:, b] - mean) * scale).astype(jnp.bfloat16)


def joint(normed_ref, weight):
    return lax.dot_general(
        normed_ref[...], weight, (((1,), (1,)), ((), ())), preferred_element_type=jnp.float32
    ).astype(jnp.bfloat16)


def hint(microseconds):
    return pl.CostEstimate(
        flops=int(microseconds * 1e9), bytes_accessed=int(microseconds * 3e6), transcendentals=0
    )


def column_kernel(found_ref, got_ref, w_in_ref, w_out_ref, out_ref, flat_ref, x_ref, normed_ref):
    rows, depth, tokens = found_ref.shape
    per = out_ref.shape[1]
    width = out_ref.shape[2]
    for s in range(rows):
        flat_ref[s * depth : (s + 1) * depth] = found_ref[s].astype(jnp.float32)
    for r in range(rows):
        x_ref[r * per : (r + 1) * per] = got_ref[r, :, :width].astype(jnp.float32)
    for i in range(0, width, 128):
        x_ref[:, i : i + 128] += jnp.transpose(flat_ref[i : i + 128])
    normalize(x_ref, normed_ref)
    joined = joint(normed_ref, w_in_ref[0])
    row_of = lax.broadcasted_iota(jnp.int32, (tokens, tokens), 0)
    col_of = lax.broadcasted_iota(jnp.int32, (tokens, tokens), 1)
    allowed = (row_of % per == col_of % per) & (row_of >= col_of)
    pieces = []
    for h in range(HEADS):
        base = 3 * HEAD * h
        query = joined[:, base : base + HEAD]
        key = joined[:, base + HEAD : base + 2 * HEAD]
        value = joined[:, base + 2 * HEAD : base + 3 * HEAD]
        scores = lax.dot_general(
            query, key, (((1,), (1,)), ((), ())), preferred_element_type=jnp.float32
        ) * (1.0 / math.sqrt(HEAD))
        scores = jnp.where(allowed, scores, -jnp.inf)
        lifted = jnp.exp(scores - jnp.max(scores, axis=1, keepdims=True))
        probs = (lifted / jnp.sum(lifted, axis=1, keepdims=True)).astype(jnp.bfloat16)
        pieces.append(
            jnp.dot(probs, value, preferred_element_type=jnp.float32).astype(jnp.bfloat16)
        )
    mixed = jnp.concatenate(pieces, axis=1)
    normed_ref[...] = (
        x_ref[...] + jnp.dot(mixed, w_out_ref[0], preferred_element_type=jnp.float32)
    ).astype(jnp.bfloat16)
    for r in range(rows):
        out_ref[r] = normed_ref[r * per : (r + 1) * per]


def column_sublayer(found, got, w_in, w_out):
    rows, depth, tokens = found.shape
    width = w_in.shape[2]
    per = tokens // rows
    return pl.pallas_call(
        column_kernel,
        out_shape=jax.ShapeDtypeStruct((rows, per, width), jnp.bfloat16),
        in_specs=[pl.BlockSpec(memory_space=pltpu.VMEM)] * 4,
        out_specs=pl.BlockSpec(memory_space=pltpu.VMEM),
        scratch_shapes=[
            pltpu.VMEM((width, tokens), jnp.float32),
            pltpu.VMEM((tokens, width), jnp.float32),
            pltpu.VMEM((tokens, width), jnp.bfloat16),
        ],
        cost_estimate=hint(20),
        compiler_params=pltpu.CompilerParams(vmem_limit_bytes=VMEM_LIMIT),
    )(found, got, w_in, w_out)


def project_kernel(resid_ref, w_in_ref, own_ref, sent_ref, x_ref, normed_ref):
    rows, per, width = resid_ref.shape
    for r in range(rows):
        x_ref[r * per : (r + 1) * per] = resid_ref[r].astype(jnp.float32)
    normalize(x_ref, normed_ref)
    joined = joint(normed_ref, w_in_ref[1])
    own_ref[...] = joined
    sent_ref[...] = jnp.concatenate(
        [joined[:, 3 * HEAD * h + HEAD : 3 * HEAD * (h + 1)] for h in range(HEADS)], axis=1
    )


def project(resid, w_in):
    rows, per, width = resid.shape
    tokens = rows * per
    return pl.pallas_call(
        project_kernel,
        out_shape=(
            jax.ShapeDtypeStruct((tokens, 3 * HEADS * HEAD), jnp.bfloat16),
            jax.ShapeDtypeStruct((tokens, 2 * HEADS * HEAD), jnp.bfloat16),
            jax.ShapeDtypeStruct((tokens, width), jnp.float32),
        ),
        in_specs=[pl.BlockSpec(memory_space=pltpu.VMEM)] * 2,
        out_specs=(pl.BlockSpec(memory_space=pltpu.VMEM),) * 3,
        scratch_shapes=[
            pltpu.VMEM((tokens, width), jnp.bfloat16),
        ],
        cost_estimate=hint(20),
        compiler_params=pltpu.CompilerParams(vmem_limit_bytes=VMEM_LIMIT),
    )(resid, w_in)


def row_kernel(own_ref, before_ref, x_ref, w_out_ref, out_ref):
    has_before = lax.axis_index("seq") > 0
    inv_root = 1.0 / math.sqrt(HEAD)
    joined = own_ref[...]
    before = before_ref[...]
    pieces = []
    for h in range(HEADS):
        base = 3 * HEAD * h
        query = joined[:, base : base + HEAD]
        key = joined[:, base + HEAD : base + 2 * HEAD].astype(jnp.float32)
        value = joined[:, base + 2 * HEAD : base + 3 * HEAD].astype(jnp.float32)
        far_key = before[:, 2 * HEAD * h : 2 * HEAD * h + HEAD]
        far_value = before[:, 2 * HEAD * h + HEAD : 2 * HEAD * (h + 1)]
        far_scores = (
            lax.dot_general(
                query, far_key, (((1,), (1,)), ((), ())), preferred_element_type=jnp.float32
            )
            * inv_root
        )
        far_scores = jnp.where(has_before, far_scores, -jnp.inf)
        own_scores = jnp.sum(query.astype(jnp.float32) * key, axis=1, keepdims=True) * inv_root
        top_score = jnp.maximum(jnp.max(far_scores, axis=1, keepdims=True), own_scores)
        far_lifted = jnp.exp(far_scores - top_score)
        own_lifted = jnp.exp(own_scores - top_score)
        total = jnp.sum(far_lifted, axis=1, keepdims=True) + own_lifted
        far_probs = (far_lifted / total).astype(jnp.bfloat16)
        own_probs = (own_lifted / total).astype(jnp.bfloat16).astype(jnp.float32)
        far_part = jnp.dot(far_probs, far_value, preferred_element_type=jnp.float32)
        pieces.append((far_part + own_probs * value).astype(jnp.bfloat16))
    mixed = jnp.concatenate(pieces, axis=1)
    out_ref[...] = (
        x_ref[...] + jnp.dot(mixed, w_out_ref[1], preferred_element_type=jnp.float32)
    ).astype(jnp.bfloat16)


def row_sublayer(own, before, x, w_out):
    return pl.pallas_call(
        row_kernel,
        out_shape=jax.ShapeDtypeStruct(x.shape, jnp.bfloat16),
        in_specs=[pl.BlockSpec(memory_space=pltpu.VMEM)] * 4,
        out_specs=pl.BlockSpec(memory_space=pltpu.VMEM),
        cost_estimate=hint(20),
        compiler_params=pltpu.CompilerParams(vmem_limit_bytes=VMEM_LIMIT),
    )(own, before, x, w_out)


def lookup_kernel(codes_ref, table_ref, out_ref):
    depth, entries = table_ref.shape
    step = entries // GROUPS
    count = out_ref.shape[0]
    padded = (depth + 7) // 8 * 8
    flipped = jnp.concatenate(
        [table_ref[...].astype(jnp.float32), jnp.zeros((padded - depth, entries), jnp.float32)],
        axis=0,
    )
    stacked = jnp.concatenate(
        [flipped[:, g * step : (g + 1) * step] for g in range(GROUPS)], axis=0
    ).astype(jnp.bfloat16)
    slots = lax.broadcasted_iota(jnp.int32, (step, 128), 0)
    for d in range(count):
        codes = codes_ref[d : d + 1, :]
        low = codes % step
        high = codes // step
        onehot = jnp.where(slots == low, 1.0, 0.0).astype(jnp.bfloat16)
        found = jnp.dot(stacked, onehot, preferred_element_type=jnp.float32)
        chosen = jnp.zeros((padded, 128), jnp.float32)
        for g in range(GROUPS):
            chosen = jnp.where(high == g, found[g * padded : (g + 1) * padded], chosen)
        out_ref[d] = chosen[:depth].astype(jnp.bfloat16)


def lookup(codes, table):
    count = codes.shape[0]
    depth = table.shape[0]
    return pl.pallas_call(
        lookup_kernel,
        out_shape=jax.ShapeDtypeStruct((count, depth, 128), jnp.bfloat16),
        in_specs=[pl.BlockSpec(memory_space=pltpu.VMEM)] * 2,
        out_specs=pl.BlockSpec(memory_space=pltpu.VMEM),
        cost_estimate=hint(60),
        compiler_params=pltpu.CompilerParams(vmem_limit_bytes=VMEM_LIMIT),
    )(codes, table)


def pack_kernel(codes_ref, position_ref, out_ref):
    rows, per, _ = out_ref.shape
    width = position_ref.shape[1]
    codes = codes_ref[...]
    digits = jnp.concatenate([codes // DIGIT, codes % DIGIT], axis=0).astype(jnp.bfloat16)
    for r in range(rows):
        out_ref[r, :, :width] = position_ref[r * per : (r + 1) * per]
        out_ref[r, :, width:] = digits


def pack(song_ids, position_table, rows):
    tokens, width = position_table.shape
    return pl.pallas_call(
        pack_kernel,
        out_shape=jax.ShapeDtypeStruct((rows, tokens // rows, width + tokens), jnp.bfloat16),
        in_specs=[pl.BlockSpec(memory_space=pltpu.VMEM)] * 2,
        out_specs=pl.BlockSpec(memory_space=pltpu.VMEM),
        cost_estimate=hint(60),
        compiler_params=pltpu.CompilerParams(vmem_limit_bytes=VMEM_LIMIT),
    )(song_ids.reshape(1, tokens), position_table)


def exchange(value):
    return lax.all_to_all(value, "seq", split_axis=0, concat_axis=0, tiled=True)


def shards(song_ids, table, position_table, w_qkv, w_out):
    rows = lax.axis_size("seq")
    tokens, width = position_table.shape
    per = tokens // rows

    got = exchange(pack(song_ids, position_table, rows))
    codes = got[:, 0, width:].astype(jnp.int32) * DIGIT + got[:, 1, width:].astype(jnp.int32)
    codes = jnp.transpose(codes.reshape(rows, rows, per), (1, 0, 2)).reshape(rows, tokens)
    found = exchange(lookup(codes, jnp.transpose(table)))
    w_in = jnp.swapaxes(w_qkv, 1, 2)
    resid = exchange(column_sublayer(found, got, w_in, w_out))
    own, sent, x = project(resid, w_in)
    before = lax.ppermute(sent, "seq", [(i, i + 1) for i in range(rows - 1)])
    return row_sublayer(own, before, x, w_out)


def solution(mesh):
    in_specs = (P(("song", "seq")), P(None, "seq"), P("seq", None), P(), P())
    out_specs = P(("song", "seq"), None)
    return jax.shard_map(shards, mesh=mesh, in_specs=in_specs, out_specs=out_specs, check_vma=False)
```

```python
import functools
import math

import jax
import jax.numpy as jnp
from jax import lax
from jax.experimental import pallas as pl
from jax.experimental.pallas import tpu as pltpu
from jax.sharding import PartitionSpec as P

HEADS = 4
HEAD = 150
GROUPS = 8
DIGIT = 64
VMEM_LIMIT = 12 * 1024 * 1024

epsilon = 1e-05


def normalize(x_ref, normed_ref):
    width = x_ref.shape[1]
    blocks = [slice(i, min(i + 128, width)) for i in range(0, width, 128)]
    total = sum(x_ref[:, b] for b in blocks)
    mean = jnp.sum(total, axis=1, keepdims=True) * (1.0 / width)
    total = jnp.zeros_like(total)
    for b in blocks:
        centered = x_ref[:, b] - mean
        total += centered * centered
    scale = lax.rsqrt(jnp.sum(total, axis=1, keepdims=True) * (1.0 / width) + epsilon)
    for b in blocks:
        normed_ref[:, b] = ((x_ref[:, b] - mean) * scale).astype(jnp.bfloat16)


def joint(normed_ref, weight):
    return lax.dot_general(
        normed_ref[...], weight, (((1,), (1,)), ((), ())), preferred_element_type=jnp.float32
    ).astype(jnp.bfloat16)


def hint(microseconds):
    return pl.CostEstimate(
        flops=int(microseconds * 1e9), bytes_accessed=int(microseconds * 3e6), transcendentals=0
    )


def column_kernel(found_ref, got_ref, w_in_ref, w_out_ref, out_ref, flat_ref, x_ref, normed_ref):
    rows, depth, tokens = found_ref.shape
    per = out_ref.shape[1]
    width = w_in_ref.shape[2]
    for s in range(rows):
        flat_ref[s * depth : (s + 1) * depth] = found_ref[s].astype(jnp.float32)
    for r in range(rows):
        x_ref[r * per : (r + 1) * per] = got_ref[r, :, :width].astype(jnp.float32)
    for i in range(0, width, 128):
        x_ref[:, i : i + 128] += jnp.transpose(flat_ref[i : i + 128])
    normalize(x_ref, normed_ref)
    joined = joint(normed_ref, w_in_ref[0])
    row_of = lax.broadcasted_iota(jnp.int32, (tokens, tokens), 0)
    col_of = lax.broadcasted_iota(jnp.int32, (tokens, tokens), 1)
    allowed = (row_of % per == col_of % per) & (row_of >= col_of)
    pieces = []
    for h in range(HEADS):
        base = 3 * HEAD * h
        query = joined[:, base : base + HEAD]
        key = joined[:, base + HEAD : base + 2 * HEAD]
        value = joined[:, base + 2 * HEAD : base + 3 * HEAD]
        scores = lax.dot_general(
            query, key, (((1,), (1,)), ((), ())), preferred_element_type=jnp.float32
        ) * (1.0 / math.sqrt(HEAD))
        scores = jnp.where(allowed, scores, -jnp.inf)
        lifted = jnp.exp(scores - jnp.max(scores, axis=1, keepdims=True))
        probs = (lifted / jnp.sum(lifted, axis=1, keepdims=True)).astype(jnp.bfloat16)
        pieces.append(
            jnp.dot(probs, value, preferred_element_type=jnp.float32).astype(jnp.bfloat16)
        )
    mixed = jnp.concatenate(pieces, axis=1)
    x_ref[...] += jnp.dot(mixed, w_out_ref[0], preferred_element_type=jnp.float32)
    normalize(x_ref, normed_ref)
    joined = joint(normed_ref, w_in_ref[1])
    keyed = jnp.concatenate(
        [joined[:, 3 * HEAD * h + HEAD : 3 * HEAD * (h + 1)] for h in range(HEADS)], axis=1
    )
    resid = x_ref[...].astype(jnp.bfloat16)
    out_ref[0, :, width:] = jnp.zeros((per, keyed.shape[1]), jnp.bfloat16)
    for r in range(rows):
        out_ref[r, :, :width] = resid[r * per : (r + 1) * per]
        if r + 1 < rows:
            out_ref[r + 1, :, width:] = keyed[r * per : (r + 1) * per]


def column_sublayer(found, got, w_in, w_out):
    rows, depth, tokens = found.shape
    width = w_in.shape[2]
    per = tokens // rows
    return pl.pallas_call(
        column_kernel,
        out_shape=jax.ShapeDtypeStruct((rows, per, width + 2 * HEADS * HEAD), jnp.bfloat16),
        in_specs=[pl.BlockSpec(memory_space=pltpu.VMEM)] * 4,
        out_specs=pl.BlockSpec(memory_space=pltpu.VMEM),
        scratch_shapes=[
            pltpu.VMEM((width, tokens), jnp.float32),
            pltpu.VMEM((tokens, width), jnp.float32),
            pltpu.VMEM((tokens, width), jnp.bfloat16),
        ],
        cost_estimate=hint(20),
        compiler_params=pltpu.CompilerParams(vmem_limit_bytes=VMEM_LIMIT),
    )(found, got, w_in, w_out)


def row_kernel(got_ref, w_in_ref, w_out_ref, out_ref, x_ref, normed_ref, before_ref):
    rows, per, _ = got_ref.shape
    width = w_in_ref.shape[2]
    has_before = lax.axis_index("seq") > 0
    inv_root = 1.0 / math.sqrt(HEAD)
    for r in range(rows):
        x_ref[r * per : (r + 1) * per] = got_ref[r, :, :width].astype(jnp.float32)
        before_ref[r * per : (r + 1) * per] = got_ref[r, :, width:]
    normalize(x_ref, normed_ref)
    joined = joint(normed_ref, w_in_ref[1])
    before = before_ref[...]
    pieces = []
    for h in range(HEADS):
        base = 3 * HEAD * h
        query = joined[:, base : base + HEAD]
        key = joined[:, base + HEAD : base + 2 * HEAD].astype(jnp.float32)
        value = joined[:, base + 2 * HEAD : base + 3 * HEAD].astype(jnp.float32)
        far_key = before[:, 2 * HEAD * h : 2 * HEAD * h + HEAD]
        far_value = before[:, 2 * HEAD * h + HEAD : 2 * HEAD * (h + 1)]
        far_scores = (
            lax.dot_general(
                query, far_key, (((1,), (1,)), ((), ())), preferred_element_type=jnp.float32
            )
            * inv_root
        )
        far_scores = jnp.where(has_before, far_scores, -jnp.inf)
        own_scores = jnp.sum(query.astype(jnp.float32) * key, axis=1, keepdims=True) * inv_root
        top_score = jnp.maximum(jnp.max(far_scores, axis=1, keepdims=True), own_scores)
        far_lifted = jnp.exp(far_scores - top_score)
        own_lifted = jnp.exp(own_scores - top_score)
        total = jnp.sum(far_lifted, axis=1, keepdims=True) + own_lifted
        far_probs = (far_lifted / total).astype(jnp.bfloat16)
        own_probs = (own_lifted / total).astype(jnp.bfloat16).astype(jnp.float32)
        far_part = jnp.dot(far_probs, far_value, preferred_element_type=jnp.float32)
        pieces.append((far_part + own_probs * value).astype(jnp.bfloat16))
    mixed = jnp.concatenate(pieces, axis=1)
    out_ref[...] = (
        x_ref[...] + jnp.dot(mixed, w_out_ref[1], preferred_element_type=jnp.float32)
    ).astype(jnp.bfloat16)


def row_sublayer(got, w_in, w_out):
    rows, per, _ = got.shape
    tokens = rows * per
    width = w_in.shape[2]
    return pl.pallas_call(
        row_kernel,
        out_shape=jax.ShapeDtypeStruct((tokens, width), jnp.bfloat16),
        in_specs=[pl.BlockSpec(memory_space=pltpu.VMEM)] * 3,
        out_specs=pl.BlockSpec(memory_space=pltpu.VMEM),
        scratch_shapes=[
            pltpu.VMEM((tokens, width), jnp.float32),
            pltpu.VMEM((tokens, width), jnp.bfloat16),
            pltpu.VMEM((tokens, 2 * HEADS * HEAD), jnp.bfloat16),
        ],
        cost_estimate=hint(20),
        compiler_params=pltpu.CompilerParams(vmem_limit_bytes=VMEM_LIMIT),
    )(got, w_in, w_out)


def lookup_kernel(codes_ref, table_ref, out_ref):
    depth, entries = table_ref.shape
    step = entries // GROUPS
    count = out_ref.shape[0]
    padded = (depth + 7) // 8 * 8
    flipped = jnp.concatenate(
        [table_ref[...].astype(jnp.float32), jnp.zeros((padded - depth, entries), jnp.float32)],
        axis=0,
    )
    stacked = jnp.concatenate(
        [flipped[:, g * step : (g + 1) * step] for g in range(GROUPS)], axis=0
    ).astype(jnp.bfloat16)
    slots = lax.broadcasted_iota(jnp.int32, (step, 128), 0)
    for d in range(count):
        codes = codes_ref[d : d + 1, :]
        low = codes % step
        high = codes // step
        onehot = jnp.where(slots == low, 1.0, 0.0).astype(jnp.bfloat16)
        found = jnp.dot(stacked, onehot, preferred_element_type=jnp.float32)
        chosen = jnp.zeros((padded, 128), jnp.float32)
        for g in range(GROUPS):
            chosen = jnp.where(high == g, found[g * padded : (g + 1) * padded], chosen)
        out_ref[d] = chosen[:depth].astype(jnp.bfloat16)


def lookup(codes, table):
    count = codes.shape[0]
    depth = table.shape[0]
    return pl.pallas_call(
        lookup_kernel,
        out_shape=jax.ShapeDtypeStruct((count, depth, 128), jnp.bfloat16),
        in_specs=[pl.BlockSpec(memory_space=pltpu.VMEM)] * 2,
        out_specs=pl.BlockSpec(memory_space=pltpu.VMEM),
        cost_estimate=hint(60),
        compiler_params=pltpu.CompilerParams(vmem_limit_bytes=VMEM_LIMIT),
    )(codes, table)


def pack_kernel(codes_ref, position_ref, out_ref):
    rows, per, _ = out_ref.shape
    width = position_ref.shape[1]
    codes = codes_ref[...]
    digits = jnp.concatenate([codes // DIGIT, codes % DIGIT], axis=0).astype(jnp.bfloat16)
    for r in range(rows):
        out_ref[r, :, :width] = position_ref[r * per : (r + 1) * per]
        out_ref[r, :, width:] = digits


def pack(song_ids, position_table, rows):
    tokens, width = position_table.shape
    return pl.pallas_call(
        pack_kernel,
        out_shape=jax.ShapeDtypeStruct((rows, tokens // rows, width + tokens), jnp.bfloat16),
        in_specs=[pl.BlockSpec(memory_space=pltpu.VMEM)] * 2,
        out_specs=pl.BlockSpec(memory_space=pltpu.VMEM),
        cost_estimate=hint(60),
        compiler_params=pltpu.CompilerParams(vmem_limit_bytes=VMEM_LIMIT),
    )(song_ids.reshape(1, tokens), position_table)


def exchange(value):
    return lax.all_to_all(value, "seq", split_axis=0, concat_axis=0, tiled=True)


def shards(song_ids, table, position_table, w_qkv, w_out):
    rows = lax.axis_size("seq")
    tokens, width = position_table.shape
    per = tokens // rows

    got = exchange(pack(song_ids, position_table, rows))
    codes = got[:, 0, width:].astype(jnp.int32) * DIGIT + got[:, 1, width:].astype(jnp.int32)
    codes = jnp.transpose(codes.reshape(rows, rows, per), (1, 0, 2)).reshape(rows, tokens)
    found = exchange(lookup(codes, jnp.transpose(table)))
    w_in = jnp.swapaxes(w_qkv, 1, 2)
    got = exchange(column_sublayer(found, got, w_in, w_out))
    return row_sublayer(got, w_in, w_out)


def solution(mesh):
    in_specs = (P(("song", "seq")), P(None, "seq"), P("seq", None), P(), P())
    out_specs = P(("song", "seq"), None)
    return jax.shard_map(shards, mesh=mesh, in_specs=in_specs, out_specs=out_specs, check_vma=False)
```

```python
import functools
import math

import jax
import jax.numpy as jnp
from jax import lax
from jax.experimental import pallas as pl
from jax.experimental.pallas import tpu as pltpu
from jax.sharding import PartitionSpec as P

HEADS = 4
HEAD = 150
GROUPS = 8
DIGIT = 64
VMEM_LIMIT = 8 * 1024 * 1024
FLIP = 3
PARTS = 4
FULL_LIMIT = 60 * 1024 * 1024
AT_ONCE = 4

epsilon = 1e-05


def normalize(x_ref, normed_ref):
    width = x_ref.shape[1]
    blocks = [slice(i, min(i + 128, width)) for i in range(0, width, 128)]
    total = sum(x_ref[:, b] for b in blocks)
    mean = jnp.sum(total, axis=1, keepdims=True) * (1.0 / width)
    total = jnp.zeros_like(total)
    for b in blocks:
        centered = x_ref[:, b] - mean
        total += centered * centered
    scale = lax.rsqrt(jnp.sum(total, axis=1, keepdims=True) * (1.0 / width) + epsilon)
    for b in blocks:
        normed_ref[:, b] = ((x_ref[:, b] - mean) * scale).astype(jnp.bfloat16)


def flip_kernel(stored_ref, out_ref):
    for j in range(out_ref.shape[0]):
        out_ref[j] = jnp.transpose(stored_ref[0, j * 128 : (j + 1) * 128])


def flip(stored, layer):
    _, columns, width = stored.shape
    return pl.pallas_call(
        flip_kernel,
        grid=(-(-columns // (128 * FLIP)),),
        out_shape=jax.ShapeDtypeStruct((-(-columns // 128), width, 128), jnp.bfloat16),
        in_specs=[pl.BlockSpec((1, 128 * FLIP, width), lambda j: (layer, j, 0))],
        out_specs=pl.BlockSpec((FLIP, width, 128), lambda j: (j, 0, 0)),
        cost_estimate=hint(10),
        compiler_params=pltpu.CompilerParams(vmem_limit_bytes=FULL_LIMIT),
    )(stored)


def joint(normed_ref, strips_ref, joined_ref):
    columns = joined_ref.shape[1]
    for j in range(0, strips_ref.shape[0], 2):
        last = min(j + 2, strips_ref.shape[0])
        weight = jnp.concatenate([strips_ref[i] for i in range(j, last)], axis=1)
        stop = min(last * 128, columns)
        joined_ref[:, j * 128 : stop] = jnp.dot(
            normed_ref[...], weight[:, : stop - j * 128], preferred_element_type=jnp.float32
        ).astype(jnp.bfloat16)


def hint(microseconds):
    return pl.CostEstimate(
        flops=int(microseconds * 1e9), bytes_accessed=int(microseconds * 3e6), transcendentals=0
    )


def column_kernel(found_ref, got_ref, w_in_ref, strips_ref, w_out_ref, out_ref, flat_ref, x_ref, normed_ref, joined_ref):
    rows, depth, tokens = found_ref.shape
    per = out_ref.shape[1]
    width = w_in_ref.shape[2]
    for s in range(rows):
        flat_ref[s * depth : (s + 1) * depth] = found_ref[s].astype(jnp.float32)
    for r in range(rows):
        x_ref[r * per : (r + 1) * per] = got_ref[r, :, :width].astype(jnp.float32)
    for i in range(0, width, 128):
        x_ref[:, i : i + 128] += jnp.transpose(flat_ref[i : i + 128])
    normalize(x_ref, normed_ref)
    joined = lax.dot_general(
        normed_ref[...], w_in_ref[0], (((1,), (1,)), ((), ())), preferred_element_type=jnp.float32
    ).astype(jnp.bfloat16)
    row_of = lax.broadcasted_iota(jnp.int32, (tokens, tokens), 0)
    col_of = lax.broadcasted_iota(jnp.int32, (tokens, tokens), 1)
    allowed = (row_of % per == col_of % per) & (row_of >= col_of)
    pieces = []
    for h in range(HEADS):
        base = 3 * HEAD * h
        query = joined[:, base : base + HEAD]
        key = joined[:, base + HEAD : base + 2 * HEAD]
        value = joined[:, base + 2 * HEAD : base + 3 * HEAD]
        scores = lax.dot_general(
            query, key, (((1,), (1,)), ((), ())), preferred_element_type=jnp.float32
        ) * (1.0 / math.sqrt(HEAD))
        scores = jnp.where(allowed, scores, -jnp.inf)
        lifted = jnp.exp(scores - jnp.max(scores, axis=1, keepdims=True))
        probs = (lifted / jnp.sum(lifted, axis=1, keepdims=True)).astype(jnp.bfloat16)
        pieces.append(
            jnp.dot(probs, value, preferred_element_type=jnp.float32).astype(jnp.bfloat16)
        )
    mixed = jnp.concatenate(pieces, axis=1)
    x_ref[...] += jnp.dot(mixed, w_out_ref[0], preferred_element_type=jnp.float32)
    normalize(x_ref, normed_ref)
    joint(normed_ref, strips_ref, joined_ref)
    joined = joined_ref[...]
    keyed = jnp.concatenate(
        [joined[:, 3 * HEAD * h + HEAD : 3 * HEAD * (h + 1)] for h in range(HEADS)], axis=1
    )
    resid = x_ref[...].astype(jnp.bfloat16)
    out_ref[0, :, width:] = jnp.zeros((per, keyed.shape[1]), jnp.bfloat16)
    for r in range(rows):
        out_ref[r, :, :width] = resid[r * per : (r + 1) * per]
        if r + 1 < rows:
            out_ref[r + 1, :, width:] = keyed[r * per : (r + 1) * per]


def column_sublayer(found, got, w_in, strips, w_out):
    rows, depth, tokens = found.shape
    width = w_in.shape[2]
    per = tokens // rows
    return pl.pallas_call(
        column_kernel,
        out_shape=jax.ShapeDtypeStruct((rows, per, width + 2 * HEADS * HEAD), jnp.bfloat16),
        in_specs=[pl.BlockSpec(memory_space=pltpu.VMEM)] * 5,
        out_specs=pl.BlockSpec(memory_space=pltpu.VMEM),
        scratch_shapes=[
            pltpu.VMEM((width, tokens), jnp.float32),
            pltpu.VMEM((tokens, width), jnp.float32),
            pltpu.VMEM((tokens, width), jnp.bfloat16),
            pltpu.VMEM((tokens, 3 * HEADS * HEAD), jnp.bfloat16),
        ],
        cost_estimate=hint(20),
        compiler_params=pltpu.CompilerParams(vmem_limit_bytes=VMEM_LIMIT),
    )(found, got, w_in, strips, w_out)


def row_kernel(got_ref, strips_ref, w_out_ref, out_ref, x_ref, normed_ref, before_ref, joined_ref):
    rows, per, _ = got_ref.shape
    width = strips_ref.shape[1]
    has_before = lax.axis_index("seq") > 0
    inv_root = 1.0 / math.sqrt(HEAD)
    for r in range(rows):
        x_ref[r * per : (r + 1) * per] = got_ref[r, :, :width].astype(jnp.float32)
        before_ref[r * per : (r + 1) * per] = got_ref[r, :, width:]
    normalize(x_ref, normed_ref)
    joint(normed_ref, strips_ref, joined_ref)
    joined = joined_ref[...]
    before = before_ref[...]
    pieces = []
    for h in range(HEADS):
        base = 3 * HEAD * h
        query = joined[:, base : base + HEAD]
        key = joined[:, base + HEAD : base + 2 * HEAD].astype(jnp.float32)
        value = joined[:, base + 2 * HEAD : base + 3 * HEAD].astype(jnp.float32)
        far_key = before[:, 2 * HEAD * h : 2 * HEAD * h + HEAD]
        far_value = before[:, 2 * HEAD * h + HEAD : 2 * HEAD * (h + 1)]
        far_scores = (
            lax.dot_general(
                query, far_key, (((1,), (1,)), ((), ())), preferred_element_type=jnp.float32
            )
            * inv_root
        )
        far_scores = jnp.where(has_before, far_scores, -jnp.inf)
        own_scores = jnp.sum(query.astype(jnp.float32) * key, axis=1, keepdims=True) * inv_root
        top_score = jnp.maximum(jnp.max(far_scores, axis=1, keepdims=True), own_scores)
        far_lifted = jnp.exp(far_scores - top_score)
        own_lifted = jnp.exp(own_scores - top_score)
        total = jnp.sum(far_lifted, axis=1, keepdims=True) + own_lifted
        far_probs = (far_lifted / total).astype(jnp.bfloat16)
        own_probs = (own_lifted / total).astype(jnp.bfloat16).astype(jnp.float32)
        far_part = jnp.dot(far_probs, far_value, preferred_element_type=jnp.float32)
        pieces.append((far_part + own_probs * value).astype(jnp.bfloat16))
    mixed = jnp.concatenate(pieces, axis=1)
    out_ref[...] = (
        x_ref[...] + jnp.dot(mixed, w_out_ref[1], preferred_element_type=jnp.float32)
    ).astype(jnp.bfloat16)


def row_sublayer(got, strips, w_out):
    rows, per, _ = got.shape
    tokens = rows * per
    width = strips.shape[1]
    return pl.pallas_call(
        row_kernel,
        out_shape=jax.ShapeDtypeStruct((tokens, width), jnp.bfloat16),
        in_specs=[pl.BlockSpec(memory_space=pltpu.VMEM)] * 3,
        out_specs=pl.BlockSpec(memory_space=pltpu.VMEM),
        scratch_shapes=[
            pltpu.VMEM((tokens, width), jnp.float32),
            pltpu.VMEM((tokens, width), jnp.bfloat16),
            pltpu.VMEM((tokens, 2 * HEADS * HEAD), jnp.bfloat16),
            pltpu.VMEM((tokens, 3 * HEADS * HEAD), jnp.bfloat16),
        ],
        cost_estimate=hint(20),
        compiler_params=pltpu.CompilerParams(vmem_limit_bytes=VMEM_LIMIT),
    )(got, strips, w_out)


def lookup_kernel(codes_ref, table_ref, out_ref):
    depth, entries = table_ref.shape
    step = entries // GROUPS
    count = out_ref.shape[0]
    padded = (depth + 7) // 8 * 8
    flipped = jnp.concatenate(
        [table_ref[...].astype(jnp.float32), jnp.zeros((padded - depth, entries), jnp.float32)],
        axis=0,
    )
    stacked = jnp.concatenate(
        [flipped[:, g * step : (g + 1) * step] for g in range(GROUPS)], axis=0
    ).astype(jnp.bfloat16)
    slots = lax.broadcasted_iota(jnp.int32, (step, AT_ONCE * 128), 0)
    for d in range(0, count, AT_ONCE):
        codes = jnp.concatenate([codes_ref[d + e : d + e + 1, :] for e in range(AT_ONCE)], axis=1)
        low = codes % step
        high = codes // step
        onehot = jnp.where(slots == low, 1.0, 0.0).astype(jnp.bfloat16)
        found = jnp.dot(stacked, onehot, preferred_element_type=jnp.float32)
        chosen = jnp.zeros((padded, AT_ONCE * 128), jnp.float32)
        for g in range(GROUPS):
            chosen = jnp.where(high == g, found[g * padded : (g + 1) * padded], chosen)
        for e in range(AT_ONCE):
            out_ref[d + e] = chosen[:depth, e * 128 : (e + 1) * 128].astype(jnp.bfloat16)


def lookup(codes, table):
    count = codes.shape[0]
    depth = table.shape[0]
    return pl.pallas_call(
        lookup_kernel,
        out_shape=jax.ShapeDtypeStruct((count, depth, 128), jnp.bfloat16),
        in_specs=[pl.BlockSpec(memory_space=pltpu.VMEM)] * 2,
        out_specs=pl.BlockSpec(memory_space=pltpu.VMEM),
        cost_estimate=hint(140),
        compiler_params=pltpu.CompilerParams(vmem_limit_bytes=VMEM_LIMIT),
    )(codes, table)


def pack_kernel(codes_hbm, position_hbm, out_hbm, codes_ref, position_ref, out_ref, sem):
    rows, per, _ = out_ref.shape
    tokens, width = position_ref.shape
    part = rows // PARTS
    fetch = [pltpu.make_async_copy(codes_hbm, codes_ref, sem.at[0])]
    for i in range(PARTS):
        span = pl.ds(i * part * per, part * per)
        fetch.append(
            pltpu.make_async_copy(position_hbm.at[span], position_ref.at[span], sem.at[1 + i])
        )
    for copy in fetch:
        copy.start()
    fetch[0].wait()
    codes = codes_ref[...]
    digits = jnp.concatenate([codes // DIGIT, codes % DIGIT], axis=0).astype(jnp.bfloat16)
    store = []
    for i in range(PARTS):
        fetch[1 + i].wait()
        for r in range(i * part, (i + 1) * part):
            out_ref[r, :, :width] = position_ref[r * per : (r + 1) * per]
            out_ref[r, :, width:] = digits
        span = pl.ds(i * part, part)
        store.append(pltpu.make_async_copy(out_ref.at[span], out_hbm.at[span], sem.at[1 + PARTS + i]))
        store[-1].start()
    for copy in store:
        copy.wait()


def pack(song_ids, position_table, rows):
    tokens, width = position_table.shape
    shape = (rows, tokens // rows, width + tokens)
    return pl.pallas_call(
        pack_kernel,
        out_shape=jax.ShapeDtypeStruct(shape, jnp.bfloat16),
        in_specs=[pl.BlockSpec(memory_space=pl.ANY)] * 2,
        out_specs=pl.BlockSpec(memory_space=pl.ANY),
        scratch_shapes=[
            pltpu.VMEM((1, tokens), jnp.int32),
            pltpu.VMEM((tokens, width), jnp.bfloat16),
            pltpu.VMEM(shape, jnp.bfloat16),
            pltpu.SemaphoreType.DMA((1 + 2 * PARTS,)),
        ],
        cost_estimate=hint(60),
        compiler_params=pltpu.CompilerParams(vmem_limit_bytes=FULL_LIMIT),
    )(song_ids.reshape(1, tokens), position_table)


def exchange(value):
    return lax.all_to_all(value, "seq", split_axis=0, concat_axis=0, tiled=True)


def shards(song_ids, table, position_table, w_qkv, w_out):
    rows = lax.axis_size("seq")
    tokens, width = position_table.shape
    per = tokens // rows

    got = exchange(pack(song_ids, position_table, rows))
    w_in = jnp.swapaxes(w_qkv, 1, 2)
    strips = flip(w_in, 1)
    got, strips = lax.optimization_barrier((got, strips))
    codes = got[:, 0, width:].astype(jnp.int32) * DIGIT + got[:, 1, width:].astype(jnp.int32)
    codes = jnp.transpose(codes.reshape(rows, rows, per), (1, 0, 2)).reshape(rows, tokens)
    found = exchange(lookup(codes, jnp.transpose(table)))
    got = exchange(column_sublayer(found, got, w_in, strips, w_out))
    return row_sublayer(got, strips, w_out)


def solution(mesh):
    in_specs = (P(("song", "seq")), P(None, "seq"), P("seq", None), P(), P())
    out_specs = P(("song", "seq"), None)
    return jax.shard_map(shards, mesh=mesh, in_specs=in_specs, out_specs=out_specs, check_vma=False)
```

```python
import functools
import math

import jax
import jax.numpy as jnp
from jax import lax
from jax.experimental import pallas as pl
from jax.experimental.pallas import tpu as pltpu
from jax.sharding import PartitionSpec as P

HEADS = 4
HEAD = 150
GROUPS = 8
DIGIT = 64
VMEM_LIMIT = 8 * 1024 * 1024
PARTS = 8
FULL_LIMIT = 60 * 1024 * 1024
AT_ONCE = 4

epsilon = 1e-05


def normalize(x_ref, normed_ref):
    width = x_ref.shape[1]
    blocks = [slice(i, min(i + 128, width)) for i in range(0, width, 128)]
    total = sum(x_ref[:, b] for b in blocks)
    mean = jnp.sum(total, axis=1, keepdims=True) * (1.0 / width)
    total = jnp.zeros_like(total)
    for b in blocks:
        centered = x_ref[:, b] - mean
        total += centered * centered
    scale = lax.rsqrt(jnp.sum(total, axis=1, keepdims=True) * (1.0 / width) + epsilon)
    for b in blocks:
        normed_ref[:, b] = ((x_ref[:, b] - mean) * scale).astype(jnp.bfloat16)


def stored_columns(start, stop):
    runs = [(2 * HEAD * h, 3 * HEAD * h + HEAD, 2 * HEAD) for h in range(HEADS)]
    runs += [(2 * HEAD * HEADS + HEAD * h, 3 * HEAD * h, HEAD) for h in range(HEADS)]
    pieces = []
    for first, where, count in runs:
        low, high = max(first, start), min(first + count, stop)
        if low < high:
            pieces.append((where + low - first, where + high - first))
    return pieces


def flip_kernel(layer, stored_hbm, strips_hbm, stored_ref, strips_ref, sem):
    columns, width = stored_ref.shape
    step = columns // PARTS // 8 * 8
    cuts = [step * i for i in range(PARTS)] + [columns]
    fetch = [
        pltpu.make_async_copy(
            stored_hbm.at[layer, low:high], stored_ref.at[low:high], sem.at[i]
        )
        for i, (low, high) in enumerate(zip(cuts, cuts[1:]))
    ]
    for copy in fetch:
        copy.start()
    ready = 0
    store = []
    for j in range(strips_ref.shape[0]):
        pieces = stored_columns(j * 128, (j + 1) * 128)
        while ready < PARTS and cuts[ready] < max(high for _, high in pieces):
            fetch[ready].wait()
            ready += 1
        rows = [stored_ref[low:high] for low, high in pieces]
        missing = 128 - sum(high - low for low, high in pieces)
        if missing:
            rows.append(jnp.zeros((missing, width), jnp.bfloat16))
        strips_ref[j] = jnp.transpose(jnp.concatenate(rows, axis=0))
        store.append(pltpu.make_async_copy(strips_ref.at[j], strips_hbm.at[j], sem.at[PARTS + j]))
        store[-1].start()
    for copy in fetch[ready:] + store:
        copy.wait()


def flip(stored, layer):
    _, columns, width = stored.shape
    shape = (-(-columns // 128), width, 128)
    return pl.pallas_call(
        functools.partial(flip_kernel, layer),
        out_shape=jax.ShapeDtypeStruct(shape, jnp.bfloat16),
        in_specs=[pl.BlockSpec(memory_space=pl.ANY)],
        out_specs=pl.BlockSpec(memory_space=pl.ANY),
        scratch_shapes=[
            pltpu.VMEM((columns, width), jnp.bfloat16),
            pltpu.VMEM(shape, jnp.bfloat16),
            pltpu.SemaphoreType.DMA((PARTS + shape[0],)),
        ],
        cost_estimate=hint(10),
        compiler_params=pltpu.CompilerParams(vmem_limit_bytes=FULL_LIMIT),
    )(stored)


def joint(normed_ref, strips_ref, joined_ref):
    columns = joined_ref.shape[1]
    for j in range(0, -(-columns // 128), 2):
        last = min(j + 2, strips_ref.shape[0])
        weight = jnp.concatenate([strips_ref[i] for i in range(j, last)], axis=1)
        stop = min(last * 128, columns)
        joined_ref[:, j * 128 : stop] = jnp.dot(
            normed_ref[...], weight[:, : stop - j * 128], preferred_element_type=jnp.float32
        ).astype(jnp.bfloat16)


def product(left, right, dims):
    return lax.dot_general(left, right, (((dims[0],), (dims[1],)), ((), ())), preferred_element_type=jnp.float32)


def hint(microseconds):
    return pl.CostEstimate(
        flops=int(microseconds * 1e9), bytes_accessed=int(microseconds * 3e6), transcendentals=0
    )


def column_kernel(found_ref, got_ref, w_in_ref, strips_ref, w_out_ref, out_ref, flat_ref, x_ref, normed_ref, keyed_ref):
    rows, depth, tokens = found_ref.shape
    per = out_ref.shape[1]
    width = w_in_ref.shape[2]
    for s in range(rows):
        flat_ref[s * depth : (s + 1) * depth] = found_ref[s].astype(jnp.float32)
    for r in range(rows):
        x_ref[r * per : (r + 1) * per] = got_ref[r, :, :width].astype(jnp.float32)
    for i in range(0, width, 128):
        x_ref[:, i : i + 128] += jnp.transpose(flat_ref[i : i + 128])
    normalize(x_ref, normed_ref)
    joined = lax.dot_general(
        normed_ref[...], w_in_ref[0], (((1,), (1,)), ((), ())), preferred_element_type=jnp.float32
    ).astype(jnp.bfloat16)
    key_of = lax.broadcasted_iota(jnp.int32, (tokens, tokens), 0)
    query_of = lax.broadcasted_iota(jnp.int32, (tokens, tokens), 1)
    allowed = (key_of % per == query_of % per) & (key_of <= query_of)
    query, key, value = (
        [joined[:, 3 * HEAD * h + HEAD * i : 3 * HEAD * h + HEAD * (i + 1)] for h in range(HEADS)]
        for i in range(3)
    )
    scores = [product(k, q, (1, 1)) * (1.0 / math.sqrt(HEAD)) for q, k in zip(query, key)]
    scores = [jnp.where(allowed, s, -jnp.inf) for s in scores]
    top = [jnp.max(s, axis=0, keepdims=True) for s in scores]
    lifted = [jnp.exp(s - m) for s, m in zip(scores, top)]
    share = [1.0 / jnp.sum(e, axis=0, keepdims=True) for e in lifted]
    probs = [(e * r).astype(jnp.bfloat16) for e, r in zip(lifted, share)]
    mixed = jnp.concatenate(
        [product(p, v, (0, 0)).astype(jnp.bfloat16) for p, v in zip(probs, value)], axis=1
    )
    x_ref[...] += jnp.dot(mixed, w_out_ref[0], preferred_element_type=jnp.float32)
    normalize(x_ref, normed_ref)
    joint(normed_ref, strips_ref, keyed_ref)
    resid = x_ref[...].astype(jnp.bfloat16)
    out_ref[0, :, width:] = jnp.zeros((per, keyed_ref.shape[1]), jnp.bfloat16)
    for r in range(rows):
        out_ref[r, :, :width] = resid[r * per : (r + 1) * per]
        if r + 1 < rows:
            out_ref[r + 1, :, width:] = keyed_ref[r * per : (r + 1) * per]


def column_sublayer(found, got, w_in, strips, w_out):
    rows, depth, tokens = found.shape
    width = w_in.shape[2]
    per = tokens // rows
    return pl.pallas_call(
        column_kernel,
        out_shape=jax.ShapeDtypeStruct((rows, per, width + 2 * HEADS * HEAD), jnp.bfloat16),
        in_specs=[pl.BlockSpec(memory_space=pltpu.VMEM)] * 5,
        out_specs=pl.BlockSpec(memory_space=pltpu.VMEM),
        scratch_shapes=[
            pltpu.VMEM((width, tokens), jnp.float32),
            pltpu.VMEM((tokens, width), jnp.float32),
            pltpu.VMEM((tokens, width), jnp.bfloat16),
            pltpu.VMEM((tokens, 2 * HEADS * HEAD), jnp.bfloat16),
        ],
        cost_estimate=hint(20),
        compiler_params=pltpu.CompilerParams(vmem_limit_bytes=VMEM_LIMIT),
    )(found, got, w_in, strips, w_out)


def row_kernel(got_ref, strips_ref, w_out_ref, out_ref, x_ref, normed_ref, before_ref, joined_ref):
    rows, per, _ = got_ref.shape
    width = strips_ref.shape[1]
    has_before = lax.axis_index("seq") > 0
    inv_root = 1.0 / math.sqrt(HEAD)
    for r in range(rows):
        x_ref[r * per : (r + 1) * per] = got_ref[r, :, :width].astype(jnp.float32)
        before_ref[r * per : (r + 1) * per] = got_ref[r, :, width:]
    normalize(x_ref, normed_ref)
    joint(normed_ref, strips_ref, joined_ref)
    joined = joined_ref[...]
    before = before_ref[...]
    tokens = joined.shape[0]
    own = lax.broadcasted_iota(jnp.int32, (tokens, tokens), 0) == lax.broadcasted_iota(
        jnp.int32, (tokens, tokens), 1
    )
    start = 2 * HEADS * HEAD
    query = [joined[:, start + HEAD * h : start + HEAD * (h + 1)] for h in range(HEADS)]
    own_key, far_key, own_value, far_value = (
        [part[:, HEAD * (2 * h + i) : HEAD * (2 * h + i + 1)] for h in range(HEADS)]
        for i in range(2)
        for part in (joined, before)
    )
    far = [product(k, q, (1, 1)) * inv_root for q, k in zip(query, far_key)]
    far = [jnp.where(has_before, s, -jnp.inf) for s in far]
    near = [product(k, q, (1, 1)) * inv_root for q, k in zip(query, own_key)]
    near = [jnp.sum(jnp.where(own, s, 0.0), axis=0, keepdims=True) for s in near]
    top = [jnp.maximum(jnp.max(f, axis=0, keepdims=True), n) for f, n in zip(far, near)]
    far = [jnp.exp(f - m) for f, m in zip(far, top)]
    near = [jnp.exp(n - m) for n, m in zip(near, top)]
    share = [1.0 / (jnp.sum(f, axis=0, keepdims=True) + n) for f, n in zip(far, near)]
    far = [(f * r).astype(jnp.bfloat16) for f, r in zip(far, share)]
    near = [jnp.where(own, n * r, 0.0).astype(jnp.bfloat16) for n, r in zip(near, share)]
    mixed = jnp.concatenate(
        [
            product(
                jnp.concatenate([far[h], near[h]], axis=0),
                jnp.concatenate([far_value[h], own_value[h]], axis=0),
                (0, 0),
            ).astype(jnp.bfloat16)
            for h in range(HEADS)
        ],
        axis=1,
    )
    out_ref[...] = (
        x_ref[...] + jnp.dot(mixed, w_out_ref[1], preferred_element_type=jnp.float32)
    ).astype(jnp.bfloat16)


def row_sublayer(got, strips, w_out):
    rows, per, _ = got.shape
    tokens = rows * per
    width = strips.shape[1]
    return pl.pallas_call(
        row_kernel,
        out_shape=jax.ShapeDtypeStruct((tokens, width), jnp.bfloat16),
        in_specs=[pl.BlockSpec(memory_space=pltpu.VMEM)] * 3,
        out_specs=pl.BlockSpec(memory_space=pltpu.VMEM),
        scratch_shapes=[
            pltpu.VMEM((tokens, width), jnp.float32),
            pltpu.VMEM((tokens, width), jnp.bfloat16),
            pltpu.VMEM((tokens, 2 * HEADS * HEAD), jnp.bfloat16),
            pltpu.VMEM((tokens, 3 * HEADS * HEAD), jnp.bfloat16),
        ],
        cost_estimate=hint(20),
        compiler_params=pltpu.CompilerParams(vmem_limit_bytes=VMEM_LIMIT),
    )(got, strips, w_out)


def lookup_kernel(codes_ref, table_ref, out_ref):
    depth, entries = table_ref.shape
    step = entries // GROUPS
    count = out_ref.shape[0]
    padded = (depth + 7) // 8 * 8
    flipped = jnp.concatenate(
        [table_ref[...].astype(jnp.float32), jnp.zeros((padded - depth, entries), jnp.float32)],
        axis=0,
    )
    stacked = jnp.concatenate(
        [flipped[:, g * step : (g + 1) * step] for g in range(GROUPS)], axis=0
    ).astype(jnp.bfloat16)
    slots = lax.broadcasted_iota(jnp.int32, (step, AT_ONCE * 128), 0)
    for d in range(0, count, AT_ONCE):
        codes = jnp.concatenate([codes_ref[d + e : d + e + 1, :] for e in range(AT_ONCE)], axis=1)
        low = codes % step
        high = codes // step
        onehot = jnp.where(slots == low, 1.0, 0.0).astype(jnp.bfloat16)
        found = jnp.dot(stacked, onehot, preferred_element_type=jnp.float32)
        chosen = jnp.zeros((padded, AT_ONCE * 128), jnp.float32)
        for g in range(GROUPS):
            chosen = jnp.where(high == g, found[g * padded : (g + 1) * padded], chosen)
        for e in range(AT_ONCE):
            out_ref[d + e] = chosen[:depth, e * 128 : (e + 1) * 128].astype(jnp.bfloat16)


def lookup(codes, table):
    count = codes.shape[0]
    depth = table.shape[0]
    return pl.pallas_call(
        lookup_kernel,
        out_shape=jax.ShapeDtypeStruct((count, depth, 128), jnp.bfloat16),
        in_specs=[pl.BlockSpec(memory_space=pltpu.VMEM)] * 2,
        out_specs=pl.BlockSpec(memory_space=pltpu.VMEM),
        cost_estimate=hint(140),
        compiler_params=pltpu.CompilerParams(vmem_limit_bytes=VMEM_LIMIT),
    )(codes, table)


def pack_kernel(codes_hbm, position_hbm, out_hbm, codes_ref, position_ref, out_ref, sem):
    rows, per, _ = out_ref.shape
    tokens, width = position_ref.shape
    part = rows // PARTS
    fetch = [pltpu.make_async_copy(codes_hbm, codes_ref, sem.at[0])]
    for i in range(PARTS):
        span = pl.ds(i * part * per, part * per)
        fetch.append(
            pltpu.make_async_copy(position_hbm.at[span], position_ref.at[span], sem.at[1 + i])
        )
    for copy in fetch:
        copy.start()
    fetch[0].wait()
    codes = codes_ref[...]
    digits = jnp.concatenate([codes // DIGIT, codes % DIGIT], axis=0).astype(jnp.bfloat16)
    store = []
    for i in range(PARTS):
        fetch[1 + i].wait()
        for r in range(i * part, (i + 1) * part):
            out_ref[r, :, :width] = position_ref[r * per : (r + 1) * per]
            out_ref[r, :, width:] = digits
        span = pl.ds(i * part, part)
        store.append(pltpu.make_async_copy(out_ref.at[span], out_hbm.at[span], sem.at[1 + PARTS + i]))
        store[-1].start()
    for copy in store:
        copy.wait()


def pack(song_ids, position_table, rows):
    tokens, width = position_table.shape
    shape = (rows, tokens // rows, width + tokens)
    return pl.pallas_call(
        pack_kernel,
        out_shape=jax.ShapeDtypeStruct(shape, jnp.bfloat16),
        in_specs=[pl.BlockSpec(memory_space=pl.ANY)] * 2,
        out_specs=pl.BlockSpec(memory_space=pl.ANY),
        scratch_shapes=[
            pltpu.VMEM((1, tokens), jnp.int32),
            pltpu.VMEM((tokens, width), jnp.bfloat16),
            pltpu.VMEM(shape, jnp.bfloat16),
            pltpu.SemaphoreType.DMA((1 + 2 * PARTS,)),
        ],
        cost_estimate=hint(60),
        compiler_params=pltpu.CompilerParams(vmem_limit_bytes=FULL_LIMIT),
    )(song_ids.reshape(1, tokens), position_table)


def exchange(value):
    return lax.all_to_all(value, "seq", split_axis=0, concat_axis=0, tiled=True)


def shards(song_ids, table, position_table, w_qkv, w_out):
    rows = lax.axis_size("seq")
    tokens, width = position_table.shape
    per = tokens // rows

    got = exchange(pack(song_ids, position_table, rows))
    w_in = jnp.swapaxes(w_qkv, 1, 2)
    strips = flip(w_in, 1)
    got, strips = lax.optimization_barrier((got, strips))
    codes = got[:, 0, width:].astype(jnp.int32) * DIGIT + got[:, 1, width:].astype(jnp.int32)
    codes = jnp.transpose(codes.reshape(rows, rows, per), (1, 0, 2)).reshape(rows, tokens)
    found = exchange(lookup(codes, jnp.transpose(table)))
    got = exchange(column_sublayer(found, got, w_in, strips, w_out))
    return row_sublayer(got, strips, w_out)


def solution(mesh):
    in_specs = (P(("song", "seq")), P(None, "seq"), P("seq", None), P(), P())
    out_specs = P(("song", "seq"), None)
    return jax.shard_map(shards, mesh=mesh, in_specs=in_specs, out_specs=out_specs, check_vma=False)
```

```python
import functools
import math

import jax
import jax.numpy as jnp
from jax import lax
from jax.experimental import pallas as pl
from jax.experimental.pallas import tpu as pltpu
from jax.sharding import PartitionSpec as P

HEADS = 4
HEAD = 150
GROUPS = 8
DIGIT = 64
VMEM_LIMIT = 8 * 1024 * 1024
PARTS = 8
OUT_STEP = 512
EARLY = (512, 1280)
FULL_LIMIT = 60 * 1024 * 1024
AT_ONCE = 4

epsilon = 1e-05


def normalize(x_ref, normed_ref):
    width = x_ref.shape[1]
    blocks = [slice(i, min(i + 128, width)) for i in range(0, width, 128)]
    total = sum(x_ref[:, b] for b in blocks)
    mean = jnp.sum(total, axis=1, keepdims=True) * (1.0 / width)
    total = jnp.zeros_like(total)
    for b in blocks:
        centered = x_ref[:, b] - mean
        total += centered * centered
    scale = lax.rsqrt(jnp.sum(total, axis=1, keepdims=True) * (1.0 / width) + epsilon)
    for b in blocks:
        normed_ref[:, b] = ((x_ref[:, b] - mean) * scale).astype(jnp.bfloat16)


def stored_columns(start, stop):
    runs = [(2 * HEAD * h, 3 * HEAD * h + HEAD, 2 * HEAD) for h in range(HEADS)]
    runs += [(2 * HEAD * HEADS + HEAD * h, 3 * HEAD * h, HEAD) for h in range(HEADS)]
    pieces = []
    for first, where, count in runs:
        low, high = max(first, start), min(first + count, stop)
        if low < high:
            pieces.append((where + low - first, where + high - first))
    return pieces


def flip_kernel(
    stored_hbm, strips_hbm, early_hbm, stored_ref, strips_ref, early_in_ref, early_ref, sem
):
    columns, width = stored_ref.shape
    step = columns // PARTS // 8 * 8
    cuts = [step * i for i in range(PARTS)] + [columns]
    fetch = [
        pltpu.make_async_copy(
            stored_hbm.at[1, low:high], stored_ref.at[low:high], sem.at[i]
        )
        for i, (low, high) in enumerate(zip(cuts, cuts[1:]))
    ]
    extra = PARTS + strips_ref.shape[0]
    early = [
        pltpu.make_async_copy(
            stored_hbm.at[0, low : low + 256], early_in_ref.at[i], sem.at[extra + i]
        )
        for i, low in enumerate(EARLY)
    ]
    for copy in fetch + early:
        copy.start()
    ready = 0
    store = []
    for j in range(strips_ref.shape[0]):
        pieces = stored_columns(j * 128, (j + 1) * 128)
        while ready < PARTS and cuts[ready] < max(high for _, high in pieces):
            fetch[ready].wait()
            ready += 1
        rows = [stored_ref[low:high] for low, high in pieces]
        missing = 128 - sum(high - low for low, high in pieces)
        if missing:
            rows.append(jnp.zeros((missing, width), jnp.bfloat16))
        strips_ref[j] = jnp.transpose(jnp.concatenate(rows, axis=0))
        store.append(pltpu.make_async_copy(strips_ref.at[j], strips_hbm.at[j], sem.at[PARTS + j]))
        store[-1].start()
    extra += len(EARLY)
    for i, copy in enumerate(early):
        copy.wait()
        early_ref[i] = jnp.transpose(early_in_ref[i])
        store.append(pltpu.make_async_copy(early_ref.at[i], early_hbm.at[i], sem.at[extra + i]))
        store[-1].start()
    for copy in fetch[ready:] + store:
        copy.wait()


def flip(stored):
    _, columns, width = stored.shape
    shape = (-(-columns // 128), width, 128)
    count = len(EARLY)
    return pl.pallas_call(
        flip_kernel,
        out_shape=(
            jax.ShapeDtypeStruct(shape, jnp.bfloat16),
            jax.ShapeDtypeStruct((count, width, 256), jnp.bfloat16),
        ),
        in_specs=[pl.BlockSpec(memory_space=pl.ANY)],
        out_specs=(pl.BlockSpec(memory_space=pl.ANY),) * 2,
        scratch_shapes=[
            pltpu.VMEM((columns, width), jnp.bfloat16),
            pltpu.VMEM(shape, jnp.bfloat16),
            pltpu.VMEM((count, 256, width), jnp.bfloat16),
            pltpu.VMEM((count, width, 256), jnp.bfloat16),
            pltpu.SemaphoreType.DMA((PARTS + shape[0] + 2 * count,)),
        ],
        cost_estimate=hint(10),
        compiler_params=pltpu.CompilerParams(vmem_limit_bytes=FULL_LIMIT),
    )(stored)


def joint(normed_ref, strips_ref, joined_ref):
    columns = joined_ref.shape[1]
    for j in range(0, -(-columns // 128), 2):
        last = min(j + 2, strips_ref.shape[0])
        weight = jnp.concatenate([strips_ref[i] for i in range(j, last)], axis=1)
        stop = min(last * 128, columns)
        joined_ref[:, j * 128 : stop] = jnp.dot(
            normed_ref[...], weight[:, : stop - j * 128], preferred_element_type=jnp.float32
        ).astype(jnp.bfloat16)


def product(left, right, dims):
    return lax.dot_general(left, right, (((dims[0],), (dims[1],)), ((), ())), preferred_element_type=jnp.float32)


def hint(microseconds):
    return pl.CostEstimate(
        flops=int(microseconds * 1e9), bytes_accessed=int(microseconds * 3e6), transcendentals=0
    )


def column_kernel(
    found_ref, got_ref, w_in_ref, strips_ref, early_ref, w_out_ref, out_ref,
    flat_ref, x_ref, normed_ref, joined_ref, keyed_ref,
):
    rows, depth, tokens = found_ref.shape
    per = out_ref.shape[1]
    width = w_in_ref.shape[2]
    for s in range(rows):
        flat_ref[s * depth : (s + 1) * depth] = found_ref[s].astype(jnp.float32)
    for r in range(rows):
        x_ref[r * per : (r + 1) * per] = got_ref[r, :, :width].astype(jnp.float32)
    for i in range(0, width, 128):
        x_ref[:, i : i + 128] += jnp.transpose(flat_ref[i : i + 128])
    normalize(x_ref, normed_ref)
    columns = joined_ref.shape[1]
    stop = 0
    for i, low in enumerate(EARLY + (columns,)):
        if stop < low:
            joined_ref[:, stop:low] = product(
                normed_ref[...], w_in_ref[0, stop:low], (1, 1)
            ).astype(jnp.bfloat16)
        if low < columns:
            joined_ref[:, low : low + 256] = product(
                normed_ref[...], early_ref[i], (1, 0)
            ).astype(jnp.bfloat16)
        stop = low + 256
    joined = joined_ref[...]
    key_of = lax.broadcasted_iota(jnp.int32, (tokens, tokens), 0)
    query_of = lax.broadcasted_iota(jnp.int32, (tokens, tokens), 1)
    allowed = (key_of % per == query_of % per) & (key_of <= query_of)
    query, key, value = (
        [joined[:, 3 * HEAD * h + HEAD * i : 3 * HEAD * h + HEAD * (i + 1)] for h in range(HEADS)]
        for i in range(3)
    )
    scores = [product(k, q, (1, 1)) * (1.0 / math.sqrt(HEAD)) for q, k in zip(query, key)]
    scores = [jnp.where(allowed, s, -jnp.inf) for s in scores]
    top = [jnp.max(s, axis=0, keepdims=True) for s in scores]
    lifted = [jnp.exp(s - m) for s, m in zip(scores, top)]
    share = [1.0 / jnp.sum(e, axis=0, keepdims=True) for e in lifted]
    probs = [(e * r).astype(jnp.bfloat16) for e, r in zip(lifted, share)]
    mixed = jnp.concatenate(
        [product(p, v, (0, 0)).astype(jnp.bfloat16) for p, v in zip(probs, value)], axis=1
    )
    for i in range(0, width, OUT_STEP):
        span = slice(i, min(i + OUT_STEP, width))
        x_ref[:, span] += jnp.dot(
            mixed, w_out_ref[0, :, span], preferred_element_type=jnp.float32
        )
    normalize(x_ref, normed_ref)
    joint(normed_ref, strips_ref, keyed_ref)
    resid = x_ref[...].astype(jnp.bfloat16)
    out_ref[0, :, width:] = jnp.zeros((per, keyed_ref.shape[1]), jnp.bfloat16)
    for r in range(rows):
        out_ref[r, :, :width] = resid[r * per : (r + 1) * per]
        if r + 1 < rows:
            out_ref[r + 1, :, width:] = keyed_ref[r * per : (r + 1) * per]


def column_sublayer(found, got, w_in, strips, early, w_out):
    rows, depth, tokens = found.shape
    width = w_in.shape[2]
    per = tokens // rows
    return pl.pallas_call(
        column_kernel,
        out_shape=jax.ShapeDtypeStruct((rows, per, width + 2 * HEADS * HEAD), jnp.bfloat16),
        in_specs=[pl.BlockSpec(memory_space=pltpu.VMEM)] * 6,
        out_specs=pl.BlockSpec(memory_space=pltpu.VMEM),
        scratch_shapes=[
            pltpu.VMEM((width, tokens), jnp.float32),
            pltpu.VMEM((tokens, width), jnp.float32),
            pltpu.VMEM((tokens, width), jnp.bfloat16),
            pltpu.VMEM((tokens, 3 * HEADS * HEAD), jnp.bfloat16),
            pltpu.VMEM((tokens, 2 * HEADS * HEAD), jnp.bfloat16),
        ],
        cost_estimate=hint(20),
        compiler_params=pltpu.CompilerParams(vmem_limit_bytes=VMEM_LIMIT),
    )(found, got, w_in, strips, early, w_out)


def row_kernel(got_ref, strips_ref, w_out_ref, out_ref, x_ref, normed_ref, before_ref, joined_ref):
    rows, per, _ = got_ref.shape
    width = strips_ref.shape[1]
    has_before = lax.axis_index("seq") > 0
    inv_root = 1.0 / math.sqrt(HEAD)
    for r in range(rows):
        x_ref[r * per : (r + 1) * per] = got_ref[r, :, :width].astype(jnp.float32)
        before_ref[r * per : (r + 1) * per] = got_ref[r, :, width:]
    normalize(x_ref, normed_ref)
    joint(normed_ref, strips_ref, joined_ref)
    joined = joined_ref[...]
    before = before_ref[...]
    tokens = joined.shape[0]
    own = lax.broadcasted_iota(jnp.int32, (tokens, tokens), 0) == lax.broadcasted_iota(
        jnp.int32, (tokens, tokens), 1
    )
    start = 2 * HEADS * HEAD
    query = [joined[:, start + HEAD * h : start + HEAD * (h + 1)] for h in range(HEADS)]
    own_key, far_key, own_value, far_value = (
        [part[:, HEAD * (2 * h + i) : HEAD * (2 * h + i + 1)] for h in range(HEADS)]
        for i in range(2)
        for part in (joined, before)
    )
    far = [product(k, q, (1, 1)) * inv_root for q, k in zip(query, far_key)]
    far = [jnp.where(has_before, s, -jnp.inf) for s in far]
    near = [product(k, q, (1, 1)) * inv_root for q, k in zip(query, own_key)]
    near = [jnp.sum(jnp.where(own, s, 0.0), axis=0, keepdims=True) for s in near]
    top = [jnp.maximum(jnp.max(f, axis=0, keepdims=True), n) for f, n in zip(far, near)]
    far = [jnp.exp(f - m) for f, m in zip(far, top)]
    near = [jnp.exp(n - m) for n, m in zip(near, top)]
    share = [1.0 / (jnp.sum(f, axis=0, keepdims=True) + n) for f, n in zip(far, near)]
    far = [(f * r).astype(jnp.bfloat16) for f, r in zip(far, share)]
    near = [jnp.where(own, n * r, 0.0).astype(jnp.bfloat16) for n, r in zip(near, share)]
    mixed = jnp.concatenate(
        [
            product(
                jnp.concatenate([far[h], near[h]], axis=0),
                jnp.concatenate([far_value[h], own_value[h]], axis=0),
                (0, 0),
            ).astype(jnp.bfloat16)
            for h in range(HEADS)
        ],
        axis=1,
    )
    for i in range(0, width, OUT_STEP):
        span = slice(i, min(i + OUT_STEP, width))
        out_ref[:, span] = (
            x_ref[:, span]
            + jnp.dot(mixed, w_out_ref[1, :, span], preferred_element_type=jnp.float32)
        ).astype(jnp.bfloat16)


def row_sublayer(got, strips, w_out):
    rows, per, _ = got.shape
    tokens = rows * per
    width = strips.shape[1]
    return pl.pallas_call(
        row_kernel,
        out_shape=jax.ShapeDtypeStruct((tokens, width), jnp.bfloat16),
        in_specs=[pl.BlockSpec(memory_space=pltpu.VMEM)] * 3,
        out_specs=pl.BlockSpec(memory_space=pltpu.VMEM),
        scratch_shapes=[
            pltpu.VMEM((tokens, width), jnp.float32),
            pltpu.VMEM((tokens, width), jnp.bfloat16),
            pltpu.VMEM((tokens, 2 * HEADS * HEAD), jnp.bfloat16),
            pltpu.VMEM((tokens, 3 * HEADS * HEAD), jnp.bfloat16),
        ],
        cost_estimate=hint(20),
        compiler_params=pltpu.CompilerParams(vmem_limit_bytes=VMEM_LIMIT),
    )(got, strips, w_out)


def lookup_kernel(codes_ref, table_ref, out_ref):
    depth, entries = table_ref.shape
    step = entries // GROUPS
    count = out_ref.shape[0]
    padded = (depth + 7) // 8 * 8
    flipped = jnp.concatenate(
        [table_ref[...].astype(jnp.float32), jnp.zeros((padded - depth, entries), jnp.float32)],
        axis=0,
    )
    stacked = jnp.concatenate(
        [flipped[:, g * step : (g + 1) * step] for g in range(GROUPS)], axis=0
    ).astype(jnp.bfloat16)
    slots = lax.broadcasted_iota(jnp.int32, (step, AT_ONCE * 128), 0)
    slots = slots.astype(jnp.float32).astype(jnp.bfloat16)
    for d in range(0, count, AT_ONCE):
        codes = jnp.concatenate([codes_ref[d + e : d + e + 1, :] for e in range(AT_ONCE)], axis=1)
        low = (codes % step).astype(jnp.float32).astype(jnp.bfloat16)
        high = codes // step
        onehot = jnp.where(slots == low, jnp.bfloat16(1), jnp.bfloat16(0))
        found = jnp.dot(stacked, onehot, preferred_element_type=jnp.float32)
        chosen = jnp.zeros((padded, AT_ONCE * 128), jnp.float32)
        for g in range(GROUPS):
            chosen = jnp.where(high == g, found[g * padded : (g + 1) * padded], chosen)
        for e in range(AT_ONCE):
            out_ref[d + e] = chosen[:depth, e * 128 : (e + 1) * 128].astype(jnp.bfloat16)


def lookup(codes, table):
    count = codes.shape[0]
    depth = table.shape[0]
    return pl.pallas_call(
        lookup_kernel,
        out_shape=jax.ShapeDtypeStruct((count, depth, 128), jnp.bfloat16),
        in_specs=[pl.BlockSpec(memory_space=pltpu.VMEM)] * 2,
        out_specs=pl.BlockSpec(memory_space=pltpu.VMEM),
        cost_estimate=hint(140),
        compiler_params=pltpu.CompilerParams(vmem_limit_bytes=VMEM_LIMIT),
    )(codes, table)


def pack_kernel(codes_hbm, position_hbm, out_hbm, codes_ref, position_ref, out_ref, sem):
    rows, per, _ = out_ref.shape
    tokens, width = position_ref.shape
    part = rows // PARTS
    fetch = [pltpu.make_async_copy(codes_hbm, codes_ref, sem.at[0])]
    for i in range(PARTS):
        span = pl.ds(i * part * per, part * per)
        fetch.append(
            pltpu.make_async_copy(position_hbm.at[span], position_ref.at[span], sem.at[1 + i])
        )
    for copy in fetch:
        copy.start()
    fetch[0].wait()
    codes = codes_ref[...]
    digits = jnp.concatenate([codes // DIGIT, codes % DIGIT], axis=0).astype(jnp.bfloat16)
    store = []
    for i in range(PARTS):
        fetch[1 + i].wait()
        for r in range(i * part, (i + 1) * part):
            out_ref[r, :, :width] = position_ref[r * per : (r + 1) * per]
            out_ref[r, :, width:] = digits
        span = pl.ds(i * part, part)
        store.append(pltpu.make_async_copy(out_ref.at[span], out_hbm.at[span], sem.at[1 + PARTS + i]))
        store[-1].start()
    for copy in store:
        copy.wait()


def pack(song_ids, position_table, rows):
    tokens, width = position_table.shape
    shape = (rows, tokens // rows, width + tokens)
    return pl.pallas_call(
        pack_kernel,
        out_shape=jax.ShapeDtypeStruct(shape, jnp.bfloat16),
        in_specs=[pl.BlockSpec(memory_space=pl.ANY)] * 2,
        out_specs=pl.BlockSpec(memory_space=pl.ANY),
        scratch_shapes=[
            pltpu.VMEM((1, tokens), jnp.int32),
            pltpu.VMEM((tokens, width), jnp.bfloat16),
            pltpu.VMEM(shape, jnp.bfloat16),
            pltpu.SemaphoreType.DMA((1 + 2 * PARTS,)),
        ],
        cost_estimate=hint(60),
        compiler_params=pltpu.CompilerParams(vmem_limit_bytes=FULL_LIMIT),
    )(song_ids.reshape(1, tokens), position_table)


def exchange(value):
    return lax.all_to_all(value, "seq", split_axis=0, concat_axis=0, tiled=True)


def shards(song_ids, table, position_table, w_qkv, w_out):
    rows = lax.axis_size("seq")
    tokens, width = position_table.shape
    per = tokens // rows

    got = exchange(pack(song_ids, position_table, rows))
    w_in = jnp.swapaxes(w_qkv, 1, 2)
    strips, early = flip(w_in)
    got, strips, early = lax.optimization_barrier((got, strips, early))
    codes = got[:, 0, width:].astype(jnp.int32) * DIGIT + got[:, 1, width:].astype(jnp.int32)
    codes = jnp.transpose(codes.reshape(rows, rows, per), (1, 0, 2)).reshape(rows, tokens)
    found = exchange(lookup(codes, jnp.transpose(table)))
    got = exchange(column_sublayer(found, got, w_in, strips, early, w_out))
    return row_sublayer(got, strips, w_out)


def solution(mesh):
    in_specs = (P(("song", "seq")), P(None, "seq"), P("seq", None), P(), P())
    out_specs = P(("song", "seq"), None)
    return jax.shard_map(shards, mesh=mesh, in_specs=in_specs, out_specs=out_specs, check_vma=False)
```

```python
import functools
import math

import jax
import jax.numpy as jnp
from jax import lax
from jax.experimental import pallas as pl
from jax.experimental.pallas import tpu as pltpu
from jax.sharding import PartitionSpec as P

HEADS = 4
HEAD = 150
GROUPS = 8
DIGIT = 64
VMEM_LIMIT = 8 * 1024 * 1024
PARTS = 8
OUT_STEP = 512
EARLY = (128, 384, 640, 896)
FULL_LIMIT = 60 * 1024 * 1024
AT_ONCE = 4

epsilon = 1e-05


def normalize(x_ref, normed_ref):
    width = x_ref.shape[1]
    blocks = [slice(i, min(i + 128, width)) for i in range(0, width, 128)]
    total = sum(x_ref[:, b] for b in blocks)
    mean = jnp.sum(total, axis=1, keepdims=True) * (1.0 / width)
    total = jnp.zeros_like(total)
    for b in blocks:
        centered = x_ref[:, b] - mean
        total += centered * centered
    scale = lax.rsqrt(jnp.sum(total, axis=1, keepdims=True) * (1.0 / width) + epsilon)
    for b in blocks:
        normed_ref[:, b] = ((x_ref[:, b] - mean) * scale).astype(jnp.bfloat16)


def stored_columns(start, stop):
    runs = [(2 * HEAD * h, 3 * HEAD * h + HEAD, 2 * HEAD) for h in range(HEADS)]
    runs += [(2 * HEAD * HEADS + HEAD * h, 3 * HEAD * h, HEAD) for h in range(HEADS)]
    pieces = []
    for first, where, count in runs:
        low, high = max(first, start), min(first + count, stop)
        if low < high:
            pieces.append((where + low - first, where + high - first))
    return pieces


def flip_kernel(
    stored_hbm, strips_hbm, early_hbm, stored_ref, strips_ref, early_in_ref, early_ref, sem
):
    columns, width = stored_ref.shape
    step = columns // PARTS // 8 * 8
    cuts = [step * i for i in range(PARTS)] + [columns]
    fetch = [
        pltpu.make_async_copy(
            stored_hbm.at[1, low:high], stored_ref.at[low:high], sem.at[i]
        )
        for i, (low, high) in enumerate(zip(cuts, cuts[1:]))
    ]
    extra = PARTS + strips_ref.shape[0]
    early = [
        pltpu.make_async_copy(
            stored_hbm.at[0, low : low + 128], early_in_ref.at[i], sem.at[extra + i]
        )
        for i, low in enumerate(EARLY)
    ]
    for copy in fetch + early:
        copy.start()
    ready = 0
    store = []
    for j in range(strips_ref.shape[0]):
        pieces = stored_columns(j * 128, (j + 1) * 128)
        while ready < PARTS and cuts[ready] < max(high for _, high in pieces):
            fetch[ready].wait()
            ready += 1
        rows = [stored_ref[low:high] for low, high in pieces]
        missing = 128 - sum(high - low for low, high in pieces)
        if missing:
            rows.append(jnp.zeros((missing, width), jnp.bfloat16))
        strips_ref[j] = jnp.transpose(jnp.concatenate(rows, axis=0))
        store.append(pltpu.make_async_copy(strips_ref.at[j], strips_hbm.at[j], sem.at[PARTS + j]))
        store[-1].start()
    extra += len(EARLY)
    for i, copy in enumerate(early):
        copy.wait()
        early_ref[i] = jnp.transpose(early_in_ref[i])
        store.append(pltpu.make_async_copy(early_ref.at[i], early_hbm.at[i], sem.at[extra + i]))
        store[-1].start()
    for copy in fetch[ready:] + store:
        copy.wait()


def flip(stored):
    _, columns, width = stored.shape
    shape = (-(-columns // 128), width, 128)
    count = len(EARLY)
    return pl.pallas_call(
        flip_kernel,
        out_shape=(
            jax.ShapeDtypeStruct(shape, jnp.bfloat16),
            jax.ShapeDtypeStruct((count, width, 128), jnp.bfloat16),
        ),
        in_specs=[pl.BlockSpec(memory_space=pl.ANY)],
        out_specs=(pl.BlockSpec(memory_space=pl.ANY),) * 2,
        scratch_shapes=[
            pltpu.VMEM((columns, width), jnp.bfloat16),
            pltpu.VMEM(shape, jnp.bfloat16),
            pltpu.VMEM((count, 128, width), jnp.bfloat16),
            pltpu.VMEM((count, width, 128), jnp.bfloat16),
            pltpu.SemaphoreType.DMA((PARTS + shape[0] + 2 * count,)),
        ],
        cost_estimate=hint(10),
        compiler_params=pltpu.CompilerParams(vmem_limit_bytes=FULL_LIMIT),
    )(stored)


def joint(normed_ref, strips_ref, joined_ref):
    columns = joined_ref.shape[1]
    for j in range(0, -(-columns // 128), 2):
        last = min(j + 2, strips_ref.shape[0])
        weight = jnp.concatenate([strips_ref[i] for i in range(j, last)], axis=1)
        stop = min(last * 128, columns)
        joined_ref[:, j * 128 : stop] = jnp.dot(
            normed_ref[...], weight[:, : stop - j * 128], preferred_element_type=jnp.float32
        ).astype(jnp.bfloat16)


def product(left, right, dims):
    return lax.dot_general(left, right, (((dims[0],), (dims[1],)), ((), ())), preferred_element_type=jnp.float32)


def hint(microseconds):
    return pl.CostEstimate(
        flops=int(microseconds * 1e9), bytes_accessed=int(microseconds * 3e6), transcendentals=0
    )


def column_kernel(
    found_ref, got_ref, w_in_ref, strips_ref, early_ref, w_out_ref, out_ref,
    flat_ref, x_ref, normed_ref, joined_ref, keyed_ref,
):
    rows, depth, tokens = found_ref.shape
    per = out_ref.shape[1]
    width = w_in_ref.shape[2]
    for s in range(rows):
        flat_ref[s * depth : (s + 1) * depth] = found_ref[s].astype(jnp.float32)
    for r in range(rows):
        x_ref[r * per : (r + 1) * per] = got_ref[r, :, :width].astype(jnp.float32)
    for i in range(0, width, 128):
        x_ref[:, i : i + 128] += jnp.transpose(flat_ref[i : i + 128])
    normalize(x_ref, normed_ref)
    for i, low in enumerate(EARLY):
        weight = jnp.concatenate(
            [jnp.transpose(w_in_ref[0, low - 128 : low]), early_ref[i]], axis=1
        )
        joined_ref[:, low - 128 : low + 128] = product(
            normed_ref[...], weight, (1, 0)
        ).astype(jnp.bfloat16)
    stop = EARLY[-1] + 128
    joined_ref[:, stop:] = product(
        normed_ref[...], w_in_ref[0, stop:], (1, 1)
    ).astype(jnp.bfloat16)
    joined = joined_ref[...]
    key_of = lax.broadcasted_iota(jnp.int32, (tokens, tokens), 0)
    query_of = lax.broadcasted_iota(jnp.int32, (tokens, tokens), 1)
    allowed = (key_of % per == query_of % per) & (key_of <= query_of)
    query, key, value = (
        [joined[:, 3 * HEAD * h + HEAD * i : 3 * HEAD * h + HEAD * (i + 1)] for h in range(HEADS)]
        for i in range(3)
    )
    scores = [product(k, q, (1, 1)) * (1.0 / math.sqrt(HEAD)) for q, k in zip(query, key)]
    scores = [jnp.where(allowed, s, -jnp.inf) for s in scores]
    top = [jnp.max(s, axis=0, keepdims=True) for s in scores]
    lifted = [jnp.exp(s - m) for s, m in zip(scores, top)]
    share = [1.0 / jnp.sum(e, axis=0, keepdims=True) for e in lifted]
    probs = [(e * r).astype(jnp.bfloat16) for e, r in zip(lifted, share)]
    mixed = jnp.concatenate(
        [product(p, v, (0, 0)).astype(jnp.bfloat16) for p, v in zip(probs, value)], axis=1
    )
    for i in range(0, width, OUT_STEP):
        span = slice(i, min(i + OUT_STEP, width))
        x_ref[:, span] += jnp.dot(
            mixed, w_out_ref[0, :, span], preferred_element_type=jnp.float32
        )
    normalize(x_ref, normed_ref)
    joint(normed_ref, strips_ref, keyed_ref)
    resid = x_ref[...].astype(jnp.bfloat16)
    out_ref[0, :, width:] = jnp.zeros((per, keyed_ref.shape[1]), jnp.bfloat16)
    for r in range(rows):
        out_ref[r, :, :width] = resid[r * per : (r + 1) * per]
        if r + 1 < rows:
            out_ref[r + 1, :, width:] = keyed_ref[r * per : (r + 1) * per]


def column_sublayer(found, got, w_in, strips, early, w_out):
    rows, depth, tokens = found.shape
    width = w_in.shape[2]
    per = tokens // rows
    return pl.pallas_call(
        column_kernel,
        out_shape=jax.ShapeDtypeStruct((rows, per, width + 2 * HEADS * HEAD), jnp.bfloat16),
        in_specs=[pl.BlockSpec(memory_space=pltpu.VMEM)] * 6,
        out_specs=pl.BlockSpec(memory_space=pltpu.VMEM),
        scratch_shapes=[
            pltpu.VMEM((width, tokens), jnp.float32),
            pltpu.VMEM((tokens, width), jnp.float32),
            pltpu.VMEM((tokens, width), jnp.bfloat16),
            pltpu.VMEM((tokens, 3 * HEADS * HEAD), jnp.bfloat16),
            pltpu.VMEM((tokens, 2 * HEADS * HEAD), jnp.bfloat16),
        ],
        cost_estimate=hint(20),
        compiler_params=pltpu.CompilerParams(vmem_limit_bytes=VMEM_LIMIT),
    )(found, got, w_in, strips, early, w_out)


def row_kernel(got_ref, strips_ref, w_out_ref, out_ref, x_ref, normed_ref, before_ref, joined_ref):
    rows, per, _ = got_ref.shape
    width = strips_ref.shape[1]
    has_before = lax.axis_index("seq") > 0
    inv_root = 1.0 / math.sqrt(HEAD)
    for r in range(rows):
        x_ref[r * per : (r + 1) * per] = got_ref[r, :, :width].astype(jnp.float32)
        before_ref[r * per : (r + 1) * per] = got_ref[r, :, width:]
    normalize(x_ref, normed_ref)
    joint(normed_ref, strips_ref, joined_ref)
    joined = joined_ref[...]
    before = before_ref[...]
    tokens = joined.shape[0]
    own = lax.broadcasted_iota(jnp.int32, (tokens, tokens), 0) == lax.broadcasted_iota(
        jnp.int32, (tokens, tokens), 1
    )
    start = 2 * HEADS * HEAD
    query = [joined[:, start + HEAD * h : start + HEAD * (h + 1)] for h in range(HEADS)]
    own_key, far_key, own_value, far_value = (
        [part[:, HEAD * (2 * h + i) : HEAD * (2 * h + i + 1)] for h in range(HEADS)]
        for i in range(2)
        for part in (joined, before)
    )
    far = [product(k, q, (1, 1)) * inv_root for q, k in zip(query, far_key)]
    far = [jnp.where(has_before, s, -jnp.inf) for s in far]
    near = [product(k, q, (1, 1)) * inv_root for q, k in zip(query, own_key)]
    near = [jnp.sum(jnp.where(own, s, 0.0), axis=0, keepdims=True) for s in near]
    top = [jnp.maximum(jnp.max(f, axis=0, keepdims=True), n) for f, n in zip(far, near)]
    far = [jnp.exp(f - m) for f, m in zip(far, top)]
    near = [jnp.exp(n - m) for n, m in zip(near, top)]
    share = [1.0 / (jnp.sum(f, axis=0, keepdims=True) + n) for f, n in zip(far, near)]
    far = [(f * r).astype(jnp.bfloat16) for f, r in zip(far, share)]
    near = [jnp.where(own, n * r, 0.0).astype(jnp.bfloat16) for n, r in zip(near, share)]
    mixed = jnp.concatenate(
        [
            product(
                jnp.concatenate([far[h], near[h]], axis=0),
                jnp.concatenate([far_value[h], own_value[h]], axis=0),
                (0, 0),
            ).astype(jnp.bfloat16)
            for h in range(HEADS)
        ],
        axis=1,
    )
    for i in range(0, width, OUT_STEP):
        span = slice(i, min(i + OUT_STEP, width))
        out_ref[:, span] = (
            x_ref[:, span]
            + jnp.dot(mixed, w_out_ref[1, :, span], preferred_element_type=jnp.float32)
        ).astype(jnp.bfloat16)


def row_sublayer(got, strips, w_out):
    rows, per, _ = got.shape
    tokens = rows * per
    width = strips.shape[1]
    return pl.pallas_call(
        row_kernel,
        out_shape=jax.ShapeDtypeStruct((tokens, width), jnp.bfloat16),
        in_specs=[pl.BlockSpec(memory_space=pltpu.VMEM)] * 3,
        out_specs=pl.BlockSpec(memory_space=pltpu.VMEM),
        scratch_shapes=[
            pltpu.VMEM((tokens, width), jnp.float32),
            pltpu.VMEM((tokens, width), jnp.bfloat16),
            pltpu.VMEM((tokens, 2 * HEADS * HEAD), jnp.bfloat16),
            pltpu.VMEM((tokens, 3 * HEADS * HEAD), jnp.bfloat16),
        ],
        cost_estimate=hint(20),
        compiler_params=pltpu.CompilerParams(vmem_limit_bytes=VMEM_LIMIT),
    )(got, strips, w_out)


def lookup_kernel(codes_ref, table_ref, out_ref):
    depth, entries = table_ref.shape
    step = entries // GROUPS
    count = out_ref.shape[0]
    padded = (depth + 7) // 8 * 8
    flipped = jnp.concatenate(
        [table_ref[...].astype(jnp.float32), jnp.zeros((padded - depth, entries), jnp.float32)],
        axis=0,
    )
    stacked = jnp.concatenate(
        [flipped[:, g * step : (g + 1) * step] for g in range(GROUPS)], axis=0
    ).astype(jnp.bfloat16)
    slots = lax.broadcasted_iota(jnp.int32, (step, AT_ONCE * 128), 0)
    slots = slots.astype(jnp.float32).astype(jnp.bfloat16)
    for d in range(0, count, AT_ONCE):
        codes = jnp.concatenate([codes_ref[d + e : d + e + 1, :] for e in range(AT_ONCE)], axis=1)
        low = (codes % step).astype(jnp.float32).astype(jnp.bfloat16)
        high = codes // step
        onehot = jnp.where(slots == low, jnp.bfloat16(1), jnp.bfloat16(0))
        found = jnp.dot(stacked, onehot, preferred_element_type=jnp.float32)
        chosen = jnp.zeros((padded, AT_ONCE * 128), jnp.float32)
        for g in range(GROUPS):
            chosen = jnp.where(high == g, found[g * padded : (g + 1) * padded], chosen)
        for e in range(AT_ONCE):
            out_ref[d + e] = chosen[:depth, e * 128 : (e + 1) * 128].astype(jnp.bfloat16)


def lookup(codes, table):
    count = codes.shape[0]
    depth = table.shape[0]
    return pl.pallas_call(
        lookup_kernel,
        out_shape=jax.ShapeDtypeStruct((count, depth, 128), jnp.bfloat16),
        in_specs=[pl.BlockSpec(memory_space=pltpu.VMEM)] * 2,
        out_specs=pl.BlockSpec(memory_space=pltpu.VMEM),
        cost_estimate=hint(140),
        compiler_params=pltpu.CompilerParams(vmem_limit_bytes=VMEM_LIMIT),
    )(codes, table)


def pack_kernel(codes_hbm, position_hbm, out_hbm, codes_ref, position_ref, out_ref, sem):
    rows, per, _ = out_ref.shape
    tokens, width = position_ref.shape
    part = rows // PARTS
    fetch = [pltpu.make_async_copy(codes_hbm, codes_ref, sem.at[0])]
    for i in range(PARTS):
        span = pl.ds(i * part * per, part * per)
        fetch.append(
            pltpu.make_async_copy(position_hbm.at[span], position_ref.at[span], sem.at[1 + i])
        )
    for copy in fetch:
        copy.start()
    fetch[0].wait()
    codes = codes_ref[...]
    digits = jnp.concatenate([codes // DIGIT, codes % DIGIT], axis=0).astype(jnp.bfloat16)
    store = []
    for i in range(PARTS):
        fetch[1 + i].wait()
        for r in range(i * part, (i + 1) * part):
            out_ref[r, :, :width] = position_ref[r * per : (r + 1) * per]
            out_ref[r, :, width:] = digits
        span = pl.ds(i * part, part)
        store.append(pltpu.make_async_copy(out_ref.at[span], out_hbm.at[span], sem.at[1 + PARTS + i]))
        store[-1].start()
    for copy in store:
        copy.wait()


def pack(song_ids, position_table, rows):
    tokens, width = position_table.shape
    shape = (rows, tokens // rows, width + tokens)
    return pl.pallas_call(
        pack_kernel,
        out_shape=jax.ShapeDtypeStruct(shape, jnp.bfloat16),
        in_specs=[pl.BlockSpec(memory_space=pl.ANY)] * 2,
        out_specs=pl.BlockSpec(memory_space=pl.ANY),
        scratch_shapes=[
            pltpu.VMEM((1, tokens), jnp.int32),
            pltpu.VMEM((tokens, width), jnp.bfloat16),
            pltpu.VMEM(shape, jnp.bfloat16),
            pltpu.SemaphoreType.DMA((1 + 2 * PARTS,)),
        ],
        cost_estimate=hint(60),
        compiler_params=pltpu.CompilerParams(vmem_limit_bytes=FULL_LIMIT),
    )(song_ids.reshape(1, tokens), position_table)


def exchange(value):
    return lax.all_to_all(value, "seq", split_axis=0, concat_axis=0, tiled=True)


def shards(song_ids, table, position_table, w_qkv, w_out):
    rows = lax.axis_size("seq")
    tokens, width = position_table.shape
    per = tokens // rows

    got = exchange(pack(song_ids, position_table, rows))
    w_in = jnp.swapaxes(w_qkv, 1, 2)
    strips, early = flip(w_in)
    got, strips, early = lax.optimization_barrier((got, strips, early))
    codes = got[:, 0, width:].astype(jnp.int32) * DIGIT + got[:, 1, width:].astype(jnp.int32)
    codes = jnp.transpose(codes.reshape(rows, rows, per), (1, 0, 2)).reshape(rows, tokens)
    found = exchange(lookup(codes, jnp.transpose(table)))
    got = exchange(column_sublayer(found, got, w_in, strips, early, w_out))
    return row_sublayer(got, strips, w_out)


def solution(mesh):
    in_specs = (P(("song", "seq")), P(None, "seq"), P("seq", None), P(), P())
    out_specs = P(("song", "seq"), None)
    return jax.shard_map(shards, mesh=mesh, in_specs=in_specs, out_specs=out_specs, check_vma=False)
```

```python
import functools
import math

import jax
import jax.numpy as jnp
from jax import lax
from jax.experimental import pallas as pl
from jax.experimental.pallas import tpu as pltpu
from jax.sharding import PartitionSpec as P

HEADS = 4
HEAD = 150
GROUPS = 8
DIGIT = 64
VMEM_LIMIT = 8 * 1024 * 1024
PARTS = 8
OUT_STEP = 512
EARLY = (128, 384, 640, 896)
FULL_LIMIT = 60 * 1024 * 1024
AT_ONCE = 4

epsilon = 1e-05


def normalize(x_ref, normed_ref):
    width = x_ref.shape[1]
    blocks = [slice(i, min(i + 128, width)) for i in range(0, width, 128)]
    total = sum(x_ref[:, b] for b in blocks)
    mean = jnp.sum(total, axis=1, keepdims=True) * (1.0 / width)
    total = jnp.zeros_like(total)
    for b in blocks:
        centered = x_ref[:, b] - mean
        total += centered * centered
    scale = lax.rsqrt(jnp.sum(total, axis=1, keepdims=True) * (1.0 / width) + epsilon)
    for b in blocks:
        normed_ref[:, b] = ((x_ref[:, b] - mean) * scale).astype(jnp.bfloat16)


def stored_columns(start, stop):
    runs = [(2 * HEAD * h, 3 * HEAD * h + HEAD, 2 * HEAD) for h in range(HEADS)]
    runs += [(2 * HEAD * HEADS + HEAD * h, 3 * HEAD * h, HEAD) for h in range(HEADS)]
    pieces = []
    for first, where, count in runs:
        low, high = max(first, start), min(first + count, stop)
        if low < high:
            pieces.append((where + low - first, where + high - first))
    return pieces


def flip_kernel(
    stored_hbm, strips_hbm, early_hbm, stored_ref, strips_ref, early_in_ref, early_ref, sem
):
    columns, width = stored_ref.shape
    step = columns // PARTS // 8 * 8
    cuts = [step * i for i in range(PARTS)] + [columns]
    fetch = [
        pltpu.make_async_copy(
            stored_hbm.at[1, low:high], stored_ref.at[low:high], sem.at[i]
        )
        for i, (low, high) in enumerate(zip(cuts, cuts[1:]))
    ]
    extra = PARTS + strips_ref.shape[0]
    early = [
        pltpu.make_async_copy(
            stored_hbm.at[0, low : low + 128], early_in_ref.at[i], sem.at[extra + i]
        )
        for i, low in enumerate(EARLY)
    ]
    for copy in fetch + early:
        copy.start()
    ready = 0
    store = []
    for j in range(strips_ref.shape[0]):
        pieces = stored_columns(j * 128, (j + 1) * 128)
        while ready < PARTS and cuts[ready] < max(high for _, high in pieces):
            fetch[ready].wait()
            ready += 1
        rows = [stored_ref[low:high] for low, high in pieces]
        missing = 128 - sum(high - low for low, high in pieces)
        if missing:
            rows.append(jnp.zeros((missing, width), jnp.bfloat16))
        strips_ref[j] = jnp.transpose(jnp.concatenate(rows, axis=0))
        store.append(pltpu.make_async_copy(strips_ref.at[j], strips_hbm.at[j], sem.at[PARTS + j]))
        store[-1].start()
    extra += len(EARLY)
    for i, copy in enumerate(early):
        copy.wait()
        early_ref[i] = jnp.transpose(early_in_ref[i])
        store.append(pltpu.make_async_copy(early_ref.at[i], early_hbm.at[i], sem.at[extra + i]))
        store[-1].start()
    for copy in fetch[ready:] + store:
        copy.wait()


def flip(stored):
    _, columns, width = stored.shape
    shape = (-(-columns // 128), width, 128)
    count = len(EARLY)
    return pl.pallas_call(
        flip_kernel,
        out_shape=(
            jax.ShapeDtypeStruct(shape, jnp.bfloat16),
            jax.ShapeDtypeStruct((count, width, 128), jnp.bfloat16),
        ),
        in_specs=[pl.BlockSpec(memory_space=pl.ANY)],
        out_specs=(pl.BlockSpec(memory_space=pl.ANY),) * 2,
        scratch_shapes=[
            pltpu.VMEM((columns, width), jnp.bfloat16),
            pltpu.VMEM(shape, jnp.bfloat16),
            pltpu.VMEM((count, 128, width), jnp.bfloat16),
            pltpu.VMEM((count, width, 128), jnp.bfloat16),
            pltpu.SemaphoreType.DMA((PARTS + shape[0] + 2 * count,)),
        ],
        cost_estimate=hint(10),
        compiler_params=pltpu.CompilerParams(vmem_limit_bytes=FULL_LIMIT),
    )(stored)


def joint(normed_ref, strips_ref, joined_ref):
    columns = joined_ref.shape[1]
    for j in range(0, -(-columns // 128), 2):
        last = min(j + 2, strips_ref.shape[0])
        weight = jnp.concatenate([strips_ref[i] for i in range(j, last)], axis=1)
        stop = min(last * 128, columns)
        joined_ref[:, j * 128 : stop] = jnp.dot(
            normed_ref[...], weight[:, : stop - j * 128], preferred_element_type=jnp.float32
        ).astype(jnp.bfloat16)


def product(left, right, dims):
    return lax.dot_general(left, right, (((dims[0],), (dims[1],)), ((), ())), preferred_element_type=jnp.float32)


def hint(microseconds):
    return pl.CostEstimate(
        flops=int(microseconds * 1e9), bytes_accessed=int(microseconds * 3e6), transcendentals=0
    )


def column_kernel(
    found_ref, got_ref, w_in_ref, strips_ref, early_ref, w_out_ref, out_ref,
    flat_ref, x_ref, normed_ref, joined_ref, keyed_ref,
):
    rows, depth, tokens = found_ref.shape
    per = out_ref.shape[1]
    width = w_in_ref.shape[2]
    for s in range(rows):
        flat_ref[s * depth : (s + 1) * depth] = found_ref[s]
    for r in range(rows):
        normed_ref[r * per : (r + 1) * per] = got_ref[r, :, :width]
    for i in range(0, width, 128):
        x_ref[:, i : i + 128] = jnp.transpose(flat_ref[i : i + 128]).astype(
            jnp.float32
        ) + normed_ref[:, i : i + 128].astype(jnp.float32)
    normalize(x_ref, normed_ref)
    for i, low in enumerate(EARLY):
        weight = jnp.concatenate(
            [jnp.transpose(w_in_ref[0, low - 128 : low]), early_ref[i]], axis=1
        )
        joined_ref[:, low - 128 : low + 128] = product(
            normed_ref[...], weight, (1, 0)
        ).astype(jnp.bfloat16)
    stop = EARLY[-1] + 128
    joined_ref[:, stop:] = product(
        normed_ref[...], w_in_ref[0, stop:], (1, 1)
    ).astype(jnp.bfloat16)
    joined = joined_ref[...]
    key_of = lax.broadcasted_iota(jnp.int32, (tokens, tokens), 0)
    query_of = lax.broadcasted_iota(jnp.int32, (tokens, tokens), 1)
    allowed = (key_of % per == query_of % per) & (key_of <= query_of)
    query, key, value = (
        [joined[:, 3 * HEAD * h + HEAD * i : 3 * HEAD * h + HEAD * (i + 1)] for h in range(HEADS)]
        for i in range(3)
    )
    scores = [product(k, q, (1, 1)) * (1.0 / math.sqrt(HEAD)) for q, k in zip(query, key)]
    scores = [jnp.where(allowed, s, -jnp.inf) for s in scores]
    top = [jnp.max(s, axis=0, keepdims=True) for s in scores]
    lifted = [jnp.exp(s - m) for s, m in zip(scores, top)]
    share = [1.0 / jnp.sum(e, axis=0, keepdims=True) for e in lifted]
    probs = [(e * r).astype(jnp.bfloat16) for e, r in zip(lifted, share)]
    mixed = jnp.concatenate(
        [product(p, v, (0, 0)).astype(jnp.bfloat16) for p, v in zip(probs, value)], axis=1
    )
    for i in range(0, width, OUT_STEP):
        span = slice(i, min(i + OUT_STEP, width))
        x_ref[:, span] += jnp.dot(
            mixed, w_out_ref[0, :, span], preferred_element_type=jnp.float32
        )
    normalize(x_ref, normed_ref)
    joint(normed_ref, strips_ref, keyed_ref)
    resid = x_ref[...].astype(jnp.bfloat16)
    out_ref[0, :, width:] = jnp.zeros((per, keyed_ref.shape[1]), jnp.bfloat16)
    for r in range(rows):
        out_ref[r, :, :width] = resid[r * per : (r + 1) * per]
        if r + 1 < rows:
            out_ref[r + 1, :, width:] = keyed_ref[r * per : (r + 1) * per]


def column_sublayer(found, got, w_in, strips, early, w_out):
    rows, depth, tokens = found.shape
    width = w_in.shape[2]
    per = tokens // rows
    return pl.pallas_call(
        column_kernel,
        out_shape=jax.ShapeDtypeStruct((rows, per, width + 2 * HEADS * HEAD), jnp.bfloat16),
        in_specs=[pl.BlockSpec(memory_space=pltpu.VMEM)] * 6,
        out_specs=pl.BlockSpec(memory_space=pltpu.VMEM),
        scratch_shapes=[
            pltpu.VMEM((width, tokens), jnp.bfloat16),
            pltpu.VMEM((tokens, width), jnp.float32),
            pltpu.VMEM((tokens, width), jnp.bfloat16),
            pltpu.VMEM((tokens, 3 * HEADS * HEAD), jnp.bfloat16),
            pltpu.VMEM((tokens, 2 * HEADS * HEAD), jnp.bfloat16),
        ],
        cost_estimate=hint(20),
        compiler_params=pltpu.CompilerParams(vmem_limit_bytes=VMEM_LIMIT),
    )(found, got, w_in, strips, early, w_out)


def row_kernel(got_ref, strips_ref, w_out_ref, out_ref, x_ref, normed_ref, before_ref, joined_ref):
    rows, per, _ = got_ref.shape
    width = strips_ref.shape[1]
    has_before = lax.axis_index("seq") > 0
    inv_root = 1.0 / math.sqrt(HEAD)
    for r in range(rows):
        normed_ref[r * per : (r + 1) * per] = got_ref[r, :, :width]
        before_ref[r * per : (r + 1) * per] = got_ref[r, :, width:]
    x_ref[...] = normed_ref[...].astype(jnp.float32)
    normalize(x_ref, normed_ref)
    joint(normed_ref, strips_ref, joined_ref)
    joined = joined_ref[...]
    before = before_ref[...]
    tokens = joined.shape[0]
    own = lax.broadcasted_iota(jnp.int32, (tokens, tokens), 0) == lax.broadcasted_iota(
        jnp.int32, (tokens, tokens), 1
    )
    start = 2 * HEADS * HEAD
    query = [joined[:, start + HEAD * h : start + HEAD * (h + 1)] for h in range(HEADS)]
    own_key, far_key, own_value, far_value = (
        [part[:, HEAD * (2 * h + i) : HEAD * (2 * h + i + 1)] for h in range(HEADS)]
        for i in range(2)
        for part in (joined, before)
    )
    far = [product(k, q, (1, 1)) * inv_root for q, k in zip(query, far_key)]
    far = [jnp.where(has_before, s, -jnp.inf) for s in far]
    near = [product(k, q, (1, 1)) * inv_root for q, k in zip(query, own_key)]
    near = [jnp.sum(jnp.where(own, s, 0.0), axis=0, keepdims=True) for s in near]
    top = [jnp.maximum(jnp.max(f, axis=0, keepdims=True), n) for f, n in zip(far, near)]
    far = [jnp.exp(f - m) for f, m in zip(far, top)]
    near = [jnp.exp(n - m) for n, m in zip(near, top)]
    share = [1.0 / (jnp.sum(f, axis=0, keepdims=True) + n) for f, n in zip(far, near)]
    far = [(f * r).astype(jnp.bfloat16) for f, r in zip(far, share)]
    near = [jnp.where(own, n * r, 0.0).astype(jnp.bfloat16) for n, r in zip(near, share)]
    mixed = jnp.concatenate(
        [
            product(
                jnp.concatenate([far[h], near[h]], axis=0),
                jnp.concatenate([far_value[h], own_value[h]], axis=0),
                (0, 0),
            ).astype(jnp.bfloat16)
            for h in range(HEADS)
        ],
        axis=1,
    )
    for i in range(0, width, OUT_STEP):
        span = slice(i, min(i + OUT_STEP, width))
        out_ref[:, span] = (
            x_ref[:, span]
            + jnp.dot(mixed, w_out_ref[1, :, span], preferred_element_type=jnp.float32)
        ).astype(jnp.bfloat16)


def row_sublayer(got, strips, w_out):
    rows, per, _ = got.shape
    tokens = rows * per
    width = strips.shape[1]
    return pl.pallas_call(
        row_kernel,
        out_shape=jax.ShapeDtypeStruct((tokens, width), jnp.bfloat16),
        in_specs=[pl.BlockSpec(memory_space=pltpu.VMEM)] * 3,
        out_specs=pl.BlockSpec(memory_space=pltpu.VMEM),
        scratch_shapes=[
            pltpu.VMEM((tokens, width), jnp.float32),
            pltpu.VMEM((tokens, width), jnp.bfloat16),
            pltpu.VMEM((tokens, 2 * HEADS * HEAD), jnp.bfloat16),
            pltpu.VMEM((tokens, 3 * HEADS * HEAD), jnp.bfloat16),
        ],
        cost_estimate=hint(20),
        compiler_params=pltpu.CompilerParams(vmem_limit_bytes=VMEM_LIMIT),
    )(got, strips, w_out)


def lookup_kernel(got_ref, table_ref, out_ref, turned_ref, codes_ref):
    depth, entries = table_ref.shape
    step = entries // GROUPS
    count = out_ref.shape[0]
    padded = (depth + 7) // 8 * 8
    flipped = jnp.concatenate(
        [table_ref[...].astype(jnp.float32), jnp.zeros((padded - depth, entries), jnp.float32)],
        axis=0,
    )
    stacked = jnp.concatenate(
        [flipped[:, g * step : (g + 1) * step] for g in range(GROUPS)], axis=0
    ).astype(jnp.bfloat16)
    rows, per, total = got_ref.shape
    tokens = rows * per
    for i in range(2):
        digits = got_ref[:, i, total - tokens :].astype(jnp.float32)
        turned_ref[i] = jnp.transpose(
            jnp.concatenate([digits, jnp.zeros((tokens - rows, tokens), jnp.float32)], axis=0)
        )
    row_of = lax.broadcasted_iota(jnp.int32, (tokens, tokens), 0)
    place_of = lax.broadcasted_iota(jnp.int32, (tokens, tokens), 1)
    moved = jnp.zeros((2 * rows, tokens), jnp.float32)
    for c in range(per):
        picked = jnp.concatenate(
            [turned_ref[i, pl.ds(c, rows, stride=per), :] for i in range(2)], axis=0
        ).astype(jnp.bfloat16)
        spread = jnp.where(place_of == per * row_of + c, 1.0, 0.0).astype(jnp.bfloat16)
        moved += jnp.dot(picked, spread, preferred_element_type=jnp.float32)
    codes_ref[...] = moved[:rows].astype(jnp.int32) * DIGIT + moved[rows:].astype(jnp.int32)
    slots = lax.broadcasted_iota(jnp.int32, (step, AT_ONCE * 128), 0)
    slots = slots.astype(jnp.float32).astype(jnp.bfloat16)
    for d in range(0, count, AT_ONCE):
        codes = jnp.concatenate([codes_ref[d + e : d + e + 1, :] for e in range(AT_ONCE)], axis=1)
        low = (codes % step).astype(jnp.float32).astype(jnp.bfloat16)
        high = codes // step
        onehot = jnp.where(slots == low, jnp.bfloat16(1), jnp.bfloat16(0))
        found = jnp.dot(stacked, onehot, preferred_element_type=jnp.float32)
        chosen = jnp.zeros((padded, AT_ONCE * 128), jnp.float32)
        for g in range(GROUPS):
            chosen = jnp.where(high == g, found[g * padded : (g + 1) * padded], chosen)
        for e in range(AT_ONCE):
            out_ref[d + e] = chosen[:depth, e * 128 : (e + 1) * 128].astype(jnp.bfloat16)


def lookup(got, table):
    count = got.shape[0]
    tokens = count * got.shape[1]
    depth = table.shape[0]
    return pl.pallas_call(
        lookup_kernel,
        out_shape=jax.ShapeDtypeStruct((count, depth, 128), jnp.bfloat16),
        in_specs=[pl.BlockSpec(memory_space=pltpu.VMEM)] * 2,
        out_specs=pl.BlockSpec(memory_space=pltpu.VMEM),
        scratch_shapes=[
            pltpu.VMEM((2, tokens, tokens), jnp.float32),
            pltpu.VMEM((count, tokens), jnp.int32),
        ],
        cost_estimate=hint(140),
        compiler_params=pltpu.CompilerParams(vmem_limit_bytes=VMEM_LIMIT),
    )(got, table)


def pack_kernel(codes_hbm, position_hbm, out_hbm, codes_ref, position_ref, out_ref, sem):
    rows, per, _ = out_ref.shape
    tokens, width = position_ref.shape
    part = rows // PARTS
    fetch = [pltpu.make_async_copy(codes_hbm, codes_ref, sem.at[0])]
    for i in range(PARTS):
        span = pl.ds(i * part * per, part * per)
        fetch.append(
            pltpu.make_async_copy(position_hbm.at[span], position_ref.at[span], sem.at[1 + i])
        )
    for copy in fetch:
        copy.start()
    fetch[0].wait()
    codes = codes_ref[...]
    digits = jnp.concatenate([codes // DIGIT, codes % DIGIT], axis=0).astype(jnp.bfloat16)
    store = []
    for i in range(PARTS):
        fetch[1 + i].wait()
        for r in range(i * part, (i + 1) * part):
            out_ref[r, :, :width] = position_ref[r * per : (r + 1) * per]
            out_ref[r, :, width:] = digits
        span = pl.ds(i * part, part)
        store.append(pltpu.make_async_copy(out_ref.at[span], out_hbm.at[span], sem.at[1 + PARTS + i]))
        store[-1].start()
    for copy in store:
        copy.wait()


def pack(song_ids, position_table, rows):
    tokens, width = position_table.shape
    shape = (rows, tokens // rows, width + tokens)
    return pl.pallas_call(
        pack_kernel,
        out_shape=jax.ShapeDtypeStruct(shape, jnp.bfloat16),
        in_specs=[pl.BlockSpec(memory_space=pl.ANY)] * 2,
        out_specs=pl.BlockSpec(memory_space=pl.ANY),
        scratch_shapes=[
            pltpu.VMEM((1, tokens), jnp.int32),
            pltpu.VMEM((tokens, width), jnp.bfloat16),
            pltpu.VMEM(shape, jnp.bfloat16),
            pltpu.SemaphoreType.DMA((1 + 2 * PARTS,)),
        ],
        cost_estimate=hint(60),
        compiler_params=pltpu.CompilerParams(vmem_limit_bytes=FULL_LIMIT),
    )(song_ids.reshape(1, tokens), position_table)


def exchange(value):
    return lax.all_to_all(value, "seq", split_axis=0, concat_axis=0, tiled=True)


def shards(song_ids, table, position_table, w_qkv, w_out):
    rows = lax.axis_size("seq")
    tokens, width = position_table.shape
    per = tokens // rows

    got = exchange(pack(song_ids, position_table, rows))
    w_in = jnp.swapaxes(w_qkv, 1, 2)
    strips, early = flip(w_in)
    got, strips, early = lax.optimization_barrier((got, strips, early))
    found = exchange(lookup(got, jnp.transpose(table)))
    got = exchange(column_sublayer(found, got, w_in, strips, early, w_out))
    return row_sublayer(got, strips, w_out)


def solution(mesh):
    in_specs = (P(("song", "seq")), P(None, "seq"), P("seq", None), P(), P())
    out_specs = P(("song", "seq"), None)
    return jax.shard_map(shards, mesh=mesh, in_specs=in_specs, out_specs=out_specs, check_vma=False)
```

```python
import functools
import math

import jax
import jax.numpy as jnp
from jax import lax
from jax.experimental import pallas as pl
from jax.experimental.pallas import tpu as pltpu
from jax.sharding import PartitionSpec as P

HEADS = 4
HEAD = 150
GROUPS = 8
DIGIT = 64
VMEM_LIMIT = 6 * 1024 * 1024
PARTS = 8
OUT_STEP = 512
EARLY = (128, 384, 640, 896, 1152, 1408)
FULL_LIMIT = 60 * 1024 * 1024
AT_ONCE = 4

epsilon = 1e-05


def normalize(x_ref, normed_ref):
    width = x_ref.shape[1]
    blocks = [slice(i, min(i + 128, width)) for i in range(0, width, 128)]
    total = sum(x_ref[:, b] for b in blocks)
    mean = jnp.sum(total, axis=1, keepdims=True) * (1.0 / width)
    total = jnp.zeros_like(total)
    for b in blocks:
        centered = x_ref[:, b] - mean
        total += centered * centered
    scale = lax.rsqrt(jnp.sum(total, axis=1, keepdims=True) * (1.0 / width) + epsilon)
    for b in blocks:
        normed_ref[:, b] = ((x_ref[:, b] - mean) * scale).astype(jnp.bfloat16)


def stored_columns(start, stop):
    runs = [(2 * HEAD * h, 3 * HEAD * h + HEAD, 2 * HEAD) for h in range(HEADS)]
    runs += [(2 * HEAD * HEADS + HEAD * h, 3 * HEAD * h, HEAD) for h in range(HEADS)]
    pieces = []
    for first, where, count in runs:
        low, high = max(first, start), min(first + count, stop)
        if low < high:
            pieces.append((where + low - first, where + high - first))
    return pieces


def flip_kernel(
    stored_hbm, strips_hbm, early_hbm, stored_ref, strips_ref, early_in_ref, early_ref, sem
):
    columns, width = stored_ref.shape
    step = columns // PARTS // 8 * 8
    cuts = [step * i for i in range(PARTS)] + [columns]
    fetch = [
        pltpu.make_async_copy(
            stored_hbm.at[1, low:high], stored_ref.at[low:high], sem.at[i]
        )
        for i, (low, high) in enumerate(zip(cuts, cuts[1:]))
    ]
    extra = PARTS + strips_ref.shape[0]
    early = [
        pltpu.make_async_copy(
            stored_hbm.at[0, low : low + 128], early_in_ref.at[i], sem.at[extra + i]
        )
        for i, low in enumerate(EARLY)
    ]
    for copy in fetch + early:
        copy.start()
    ready = 0
    store = []
    for j in range(strips_ref.shape[0]):
        pieces = stored_columns(j * 128, (j + 1) * 128)
        while ready < PARTS and cuts[ready] < max(high for _, high in pieces):
            fetch[ready].wait()
            ready += 1
        rows = [stored_ref[low:high] for low, high in pieces]
        missing = 128 - sum(high - low for low, high in pieces)
        if missing:
            rows.append(jnp.zeros((missing, width), jnp.bfloat16))
        strips_ref[j] = jnp.transpose(jnp.concatenate(rows, axis=0))
        store.append(pltpu.make_async_copy(strips_ref.at[j], strips_hbm.at[j], sem.at[PARTS + j]))
        store[-1].start()
    extra += len(EARLY)
    for i, copy in enumerate(early):
        copy.wait()
        early_ref[i] = jnp.transpose(early_in_ref[i])
        store.append(pltpu.make_async_copy(early_ref.at[i], early_hbm.at[i], sem.at[extra + i]))
        store[-1].start()
    for copy in fetch[ready:] + store:
        copy.wait()


def flip(stored):
    _, columns, width = stored.shape
    shape = (-(-columns // 128), width, 128)
    count = len(EARLY)
    return pl.pallas_call(
        flip_kernel,
        out_shape=(
            jax.ShapeDtypeStruct(shape, jnp.bfloat16),
            jax.ShapeDtypeStruct((count, width, 128), jnp.bfloat16),
        ),
        in_specs=[pl.BlockSpec(memory_space=pl.ANY)],
        out_specs=(pl.BlockSpec(memory_space=pl.ANY),) * 2,
        scratch_shapes=[
            pltpu.VMEM((columns, width), jnp.bfloat16),
            pltpu.VMEM(shape, jnp.bfloat16),
            pltpu.VMEM((count, 128, width), jnp.bfloat16),
            pltpu.VMEM((count, width, 128), jnp.bfloat16),
            pltpu.SemaphoreType.DMA((PARTS + shape[0] + 2 * count,)),
        ],
        cost_estimate=hint(10),
        compiler_params=pltpu.CompilerParams(vmem_limit_bytes=FULL_LIMIT),
    )(stored)


def joint(normed_ref, strips_ref, joined_ref):
    columns = joined_ref.shape[1]
    for j in range(0, -(-columns // 128), 2):
        last = min(j + 2, strips_ref.shape[0])
        weight = jnp.concatenate([strips_ref[i] for i in range(j, last)], axis=1)
        stop = min(last * 128, columns)
        joined_ref[:, j * 128 : stop] = jnp.dot(
            normed_ref[...], weight[:, : stop - j * 128], preferred_element_type=jnp.float32
        ).astype(jnp.bfloat16)


def product(left, right, dims):
    return lax.dot_general(left, right, (((dims[0],), (dims[1],)), ((), ())), preferred_element_type=jnp.float32)


def hint(microseconds):
    return pl.CostEstimate(
        flops=int(microseconds * 1e9), bytes_accessed=int(microseconds * 3e6), transcendentals=0
    )


def column_kernel(
    found_ref, got_ref, w_in_ref, strips_ref, early_ref, w_out_ref, out_ref,
    flat_ref, x_ref, normed_ref, joined_ref, keyed_ref,
):
    rows, depth, tokens = found_ref.shape
    per = out_ref.shape[1]
    width = w_in_ref.shape[2]
    for s in range(rows):
        flat_ref[s * depth : (s + 1) * depth] = found_ref[s]
    for r in range(rows):
        normed_ref[r * per : (r + 1) * per] = got_ref[r, :, :width]
    for i in range(0, width, 128):
        x_ref[:, i : i + 128] = jnp.transpose(flat_ref[i : i + 128]).astype(
            jnp.float32
        ) + normed_ref[:, i : i + 128].astype(jnp.float32)
    normalize(x_ref, normed_ref)
    for i, low in enumerate(EARLY):
        weight = jnp.concatenate(
            [jnp.transpose(w_in_ref[0, low - 128 : low]), early_ref[i]], axis=1
        )
        joined_ref[:, low - 128 : low + 128] = product(
            normed_ref[...], weight, (1, 0)
        ).astype(jnp.bfloat16)
    stop = EARLY[-1] + 128
    joined_ref[:, stop:] = product(
        normed_ref[...], w_in_ref[0, stop:], (1, 1)
    ).astype(jnp.bfloat16)
    joined = joined_ref[...]
    key_of = lax.broadcasted_iota(jnp.int32, (tokens, tokens), 0)
    query_of = lax.broadcasted_iota(jnp.int32, (tokens, tokens), 1)
    allowed = (key_of % per == query_of % per) & (key_of <= query_of)
    query, key, value = (
        [joined[:, 3 * HEAD * h + HEAD * i : 3 * HEAD * h + HEAD * (i + 1)] for h in range(HEADS)]
        for i in range(3)
    )
    scores = [product(k, q, (1, 1)) * (1.0 / math.sqrt(HEAD)) for q, k in zip(query, key)]
    scores = [jnp.where(allowed, s, -jnp.inf) for s in scores]
    top = [jnp.max(s, axis=0, keepdims=True) for s in scores]
    lifted = [jnp.exp(s - m) for s, m in zip(scores, top)]
    share = [1.0 / jnp.sum(e, axis=0, keepdims=True) for e in lifted]
    probs = [(e * r).astype(jnp.bfloat16) for e, r in zip(lifted, share)]
    mixed = jnp.concatenate(
        [product(p, v, (0, 0)).astype(jnp.bfloat16) for p, v in zip(probs, value)], axis=1
    )
    for i in range(0, width, OUT_STEP):
        span = slice(i, min(i + OUT_STEP, width))
        x_ref[:, span] += jnp.dot(
            mixed, w_out_ref[0, :, span], preferred_element_type=jnp.float32
        )
    normalize(x_ref, normed_ref)
    joint(normed_ref, strips_ref, keyed_ref)
    resid = x_ref[...].astype(jnp.bfloat16)
    out_ref[0, :, width:] = jnp.zeros((per, keyed_ref.shape[1]), jnp.bfloat16)
    for r in range(rows):
        out_ref[r, :, :width] = resid[r * per : (r + 1) * per]
        if r + 1 < rows:
            out_ref[r + 1, :, width:] = keyed_ref[r * per : (r + 1) * per]


def column_sublayer(found, got, w_in, strips, early, w_out):
    rows, depth, tokens = found.shape
    width = w_in.shape[2]
    per = tokens // rows
    return pl.pallas_call(
        column_kernel,
        out_shape=jax.ShapeDtypeStruct((rows, per, width + 2 * HEADS * HEAD), jnp.bfloat16),
        in_specs=[pl.BlockSpec(memory_space=pltpu.VMEM)] * 6,
        out_specs=pl.BlockSpec(memory_space=pltpu.VMEM),
        scratch_shapes=[
            pltpu.VMEM((width, tokens), jnp.bfloat16),
            pltpu.VMEM((tokens, width), jnp.float32),
            pltpu.VMEM((tokens, width), jnp.bfloat16),
            pltpu.VMEM((tokens, 3 * HEADS * HEAD), jnp.bfloat16),
            pltpu.VMEM((tokens, 2 * HEADS * HEAD), jnp.bfloat16),
        ],
        cost_estimate=hint(20),
        compiler_params=pltpu.CompilerParams(vmem_limit_bytes=VMEM_LIMIT),
    )(found, got, w_in, strips, early, w_out)


def row_kernel(got_ref, strips_ref, w_out_ref, out_ref, x_ref, normed_ref, before_ref, joined_ref):
    rows, per, _ = got_ref.shape
    width = strips_ref.shape[1]
    has_before = lax.axis_index("seq") > 0
    inv_root = 1.0 / math.sqrt(HEAD)
    for r in range(rows):
        normed_ref[r * per : (r + 1) * per] = got_ref[r, :, :width]
        before_ref[r * per : (r + 1) * per] = got_ref[r, :, width:]
    x_ref[...] = normed_ref[...].astype(jnp.float32)
    normalize(x_ref, normed_ref)
    joint(normed_ref, strips_ref, joined_ref)
    joined = joined_ref[...]
    before = before_ref[...]
    tokens = joined.shape[0]
    own = lax.broadcasted_iota(jnp.int32, (tokens, tokens), 0) == lax.broadcasted_iota(
        jnp.int32, (tokens, tokens), 1
    )
    start = 2 * HEADS * HEAD
    query = [joined[:, start + HEAD * h : start + HEAD * (h + 1)] for h in range(HEADS)]
    own_key, far_key, own_value, far_value = (
        [part[:, HEAD * (2 * h + i) : HEAD * (2 * h + i + 1)] for h in range(HEADS)]
        for i in range(2)
        for part in (joined, before)
    )
    far = [product(k, q, (1, 1)) * inv_root for q, k in zip(query, far_key)]
    far = [jnp.where(has_before, s, -jnp.inf) for s in far]
    near = [product(k, q, (1, 1)) * inv_root for q, k in zip(query, own_key)]
    near = [jnp.sum(jnp.where(own, s, 0.0), axis=0, keepdims=True) for s in near]
    top = [jnp.maximum(jnp.max(f, axis=0, keepdims=True), n) for f, n in zip(far, near)]
    far = [jnp.exp(f - m) for f, m in zip(far, top)]
    near = [jnp.exp(n - m) for n, m in zip(near, top)]
    share = [1.0 / (jnp.sum(f, axis=0, keepdims=True) + n) for f, n in zip(far, near)]
    far = [(f * r).astype(jnp.bfloat16) for f, r in zip(far, share)]
    near = [jnp.where(own, n * r, 0.0).astype(jnp.bfloat16) for n, r in zip(near, share)]
    mixed = jnp.concatenate(
        [
            product(
                jnp.concatenate([far[h], near[h]], axis=0),
                jnp.concatenate([far_value[h], own_value[h]], axis=0),
                (0, 0),
            ).astype(jnp.bfloat16)
            for h in range(HEADS)
        ],
        axis=1,
    )
    for i in range(0, width, OUT_STEP):
        span = slice(i, min(i + OUT_STEP, width))
        out_ref[:, span] = (
            x_ref[:, span]
            + jnp.dot(mixed, w_out_ref[1, :, span], preferred_element_type=jnp.float32)
        ).astype(jnp.bfloat16)


def row_sublayer(got, strips, w_out):
    rows, per, _ = got.shape
    tokens = rows * per
    width = strips.shape[1]
    return pl.pallas_call(
        row_kernel,
        out_shape=jax.ShapeDtypeStruct((tokens, width), jnp.bfloat16),
        in_specs=[pl.BlockSpec(memory_space=pltpu.VMEM)] * 3,
        out_specs=pl.BlockSpec(memory_space=pltpu.VMEM),
        scratch_shapes=[
            pltpu.VMEM((tokens, width), jnp.float32),
            pltpu.VMEM((tokens, width), jnp.bfloat16),
            pltpu.VMEM((tokens, 2 * HEADS * HEAD), jnp.bfloat16),
            pltpu.VMEM((tokens, 3 * HEADS * HEAD), jnp.bfloat16),
        ],
        cost_estimate=hint(20),
        compiler_params=pltpu.CompilerParams(vmem_limit_bytes=VMEM_LIMIT),
    )(got, strips, w_out)


def lookup_kernel(got_ref, table_ref, out_ref, turned_ref, codes_ref):
    depth, entries = table_ref.shape
    step = entries // GROUPS
    count = out_ref.shape[0]
    padded = (depth + 7) // 8 * 8
    flipped = jnp.concatenate(
        [table_ref[...].astype(jnp.float32), jnp.zeros((padded - depth, entries), jnp.float32)],
        axis=0,
    )
    stacked = jnp.concatenate(
        [flipped[:, g * step : (g + 1) * step] for g in range(GROUPS)], axis=0
    ).astype(jnp.bfloat16)
    rows, per, total = got_ref.shape
    tokens = rows * per
    for i in range(2):
        digits = got_ref[:, i, total - tokens :].astype(jnp.float32)
        turned_ref[i] = jnp.transpose(
            jnp.concatenate([digits, jnp.zeros((tokens - rows, tokens), jnp.float32)], axis=0)
        )
    row_of = lax.broadcasted_iota(jnp.int32, (tokens, tokens), 0)
    place_of = lax.broadcasted_iota(jnp.int32, (tokens, tokens), 1)
    moved = jnp.zeros((2 * rows, tokens), jnp.float32)
    for c in range(per):
        picked = jnp.concatenate(
            [turned_ref[i, pl.ds(c, rows, stride=per), :] for i in range(2)], axis=0
        ).astype(jnp.bfloat16)
        spread = jnp.where(place_of == per * row_of + c, 1.0, 0.0).astype(jnp.bfloat16)
        moved += jnp.dot(picked, spread, preferred_element_type=jnp.float32)
    codes_ref[...] = moved[:rows].astype(jnp.int32) * DIGIT + moved[rows:].astype(jnp.int32)
    slots = lax.broadcasted_iota(jnp.int32, (step, AT_ONCE * 128), 0)
    slots = slots.astype(jnp.float32).astype(jnp.bfloat16)
    for d in range(0, count, AT_ONCE):
        codes = jnp.concatenate([codes_ref[d + e : d + e + 1, :] for e in range(AT_ONCE)], axis=1)
        low = (codes % step).astype(jnp.float32).astype(jnp.bfloat16)
        high = codes // step
        onehot = jnp.where(slots == low, jnp.bfloat16(1), jnp.bfloat16(0))
        found = jnp.dot(stacked, onehot, preferred_element_type=jnp.float32)
        chosen = jnp.zeros((padded, AT_ONCE * 128), jnp.float32)
        for g in range(GROUPS):
            chosen = jnp.where(high == g, found[g * padded : (g + 1) * padded], chosen)
        for e in range(AT_ONCE):
            out_ref[d + e] = chosen[:depth, e * 128 : (e + 1) * 128].astype(jnp.bfloat16)


def lookup(got, table):
    count = got.shape[0]
    tokens = count * got.shape[1]
    depth = table.shape[0]
    return pl.pallas_call(
        lookup_kernel,
        out_shape=jax.ShapeDtypeStruct((count, depth, 128), jnp.bfloat16),
        in_specs=[pl.BlockSpec(memory_space=pltpu.VMEM)] * 2,
        out_specs=pl.BlockSpec(memory_space=pltpu.VMEM),
        scratch_shapes=[
            pltpu.VMEM((2, tokens, tokens), jnp.float32),
            pltpu.VMEM((count, tokens), jnp.int32),
        ],
        cost_estimate=hint(140),
        compiler_params=pltpu.CompilerParams(vmem_limit_bytes=VMEM_LIMIT),
    )(got, table)


def pack_kernel(codes_hbm, position_hbm, out_hbm, codes_ref, position_ref, out_ref, sem):
    rows, per, _ = out_ref.shape
    tokens, width = position_ref.shape
    part = rows // PARTS
    fetch = [pltpu.make_async_copy(codes_hbm, codes_ref, sem.at[0])]
    for i in range(PARTS):
        span = pl.ds(i * part * per, part * per)
        fetch.append(
            pltpu.make_async_copy(position_hbm.at[span], position_ref.at[span], sem.at[1 + i])
        )
    for copy in fetch:
        copy.start()
    fetch[0].wait()
    codes = codes_ref[...]
    digits = jnp.concatenate([codes // DIGIT, codes % DIGIT], axis=0).astype(jnp.bfloat16)
    store = []
    for i in range(PARTS):
        fetch[1 + i].wait()
        for r in range(i * part, (i + 1) * part):
            out_ref[r, :, :width] = position_ref[r * per : (r + 1) * per]
            out_ref[r, :, width:] = digits
        span = pl.ds(i * part, part)
        store.append(pltpu.make_async_copy(out_ref.at[span], out_hbm.at[span], sem.at[1 + PARTS + i]))
        store[-1].start()
    for copy in store:
        copy.wait()


def pack(song_ids, position_table, rows):
    tokens, width = position_table.shape
    shape = (rows, tokens // rows, width + tokens)
    return pl.pallas_call(
        pack_kernel,
        out_shape=jax.ShapeDtypeStruct(shape, jnp.bfloat16),
        in_specs=[pl.BlockSpec(memory_space=pl.ANY)] * 2,
        out_specs=pl.BlockSpec(memory_space=pl.ANY),
        scratch_shapes=[
            pltpu.VMEM((1, tokens), jnp.int32),
            pltpu.VMEM((tokens, width), jnp.bfloat16),
            pltpu.VMEM(shape, jnp.bfloat16),
            pltpu.SemaphoreType.DMA((1 + 2 * PARTS,)),
        ],
        cost_estimate=hint(60),
        compiler_params=pltpu.CompilerParams(vmem_limit_bytes=FULL_LIMIT),
    )(song_ids.reshape(1, tokens), position_table)


def exchange(value):
    return lax.all_to_all(value, "seq", split_axis=0, concat_axis=0, tiled=True)


def shards(song_ids, table, position_table, w_qkv, w_out):
    rows = lax.axis_size("seq")
    tokens, width = position_table.shape
    per = tokens // rows

    got = exchange(pack(song_ids, position_table, rows))
    w_in = jnp.swapaxes(w_qkv, 1, 2)
    strips, early = flip(w_in)
    got, strips, early = lax.optimization_barrier((got, strips, early))
    found = exchange(lookup(got, jnp.transpose(table)))
    got = exchange(column_sublayer(found, got, w_in, strips, early, w_out))
    return row_sublayer(got, strips, w_out)


def solution(mesh):
    in_specs = (P(("song", "seq")), P(None, "seq"), P("seq", None), P(), P())
    out_specs = P(("song", "seq"), None)
    return jax.shard_map(shards, mesh=mesh, in_specs=in_specs, out_specs=out_specs, check_vma=False)
```

```python
import functools
import math

import jax
import jax.numpy as jnp
from jax import lax
from jax.experimental import pallas as pl
from jax.experimental.pallas import tpu as pltpu
from jax.sharding import PartitionSpec as P

HEADS = 4
HEAD = 150
GROUPS = 8
DIGIT = 64
VMEM_LIMIT = 6 * 1024 * 1024
PARTS = 8
OUT_STEP = 256
EARLY = (128, 384, 640, 896, 1152, 1408)
FULL_LIMIT = 60 * 1024 * 1024
AT_ONCE = 4

epsilon = 1e-05


def normalize(x_ref, normed_ref):
    width = x_ref.shape[1]
    blocks = [slice(i, min(i + 128, width)) for i in range(0, width, 128)]
    total = sum(x_ref[:, b] for b in blocks)
    mean = jnp.sum(total, axis=1, keepdims=True) * (1.0 / width)
    total = jnp.zeros_like(total)
    for b in blocks:
        centered = x_ref[:, b] - mean
        total += centered * centered
    scale = lax.rsqrt(jnp.sum(total, axis=1, keepdims=True) * (1.0 / width) + epsilon)
    for b in blocks:
        normed_ref[:, b] = ((x_ref[:, b] - mean) * scale).astype(jnp.bfloat16)


def stored_columns(start, stop):
    runs = [(2 * HEAD * h, 3 * HEAD * h + HEAD, 2 * HEAD) for h in range(HEADS)]
    runs += [(2 * HEAD * HEADS + HEAD * h, 3 * HEAD * h, HEAD) for h in range(HEADS)]
    pieces = []
    for first, where, count in runs:
        low, high = max(first, start), min(first + count, stop)
        if low < high:
            pieces.append((where + low - first, where + high - first))
    return pieces


def flip_kernel(
    stored_hbm, strips_hbm, early_hbm, stored_ref, strips_ref, early_in_ref, early_ref, sem
):
    columns, width = stored_ref.shape
    step = columns // PARTS // 8 * 8
    cuts = [step * i for i in range(PARTS)] + [columns]
    fetch = [
        pltpu.make_async_copy(
            stored_hbm.at[1, low:high], stored_ref.at[low:high], sem.at[i]
        )
        for i, (low, high) in enumerate(zip(cuts, cuts[1:]))
    ]
    extra = PARTS + strips_ref.shape[0]
    early = [
        pltpu.make_async_copy(
            stored_hbm.at[0, low : low + 128], early_in_ref.at[i], sem.at[extra + i]
        )
        for i, low in enumerate(EARLY)
    ]
    for copy in fetch + early:
        copy.start()
    ready = 0
    store = []
    for j in range(strips_ref.shape[0]):
        pieces = stored_columns(j * 128, (j + 1) * 128)
        while ready < PARTS and cuts[ready] < max(high for _, high in pieces):
            fetch[ready].wait()
            ready += 1
        rows = [stored_ref[low:high] for low, high in pieces]
        missing = 128 - sum(high - low for low, high in pieces)
        if missing:
            rows.append(jnp.zeros((missing, width), jnp.bfloat16))
        strips_ref[j] = jnp.transpose(jnp.concatenate(rows, axis=0))
        store.append(pltpu.make_async_copy(strips_ref.at[j], strips_hbm.at[j], sem.at[PARTS + j]))
        store[-1].start()
    extra += len(EARLY)
    for i, copy in enumerate(early):
        copy.wait()
        early_ref[i] = jnp.transpose(early_in_ref[i])
        store.append(pltpu.make_async_copy(early_ref.at[i], early_hbm.at[i], sem.at[extra + i]))
        store[-1].start()
    for copy in fetch[ready:] + store:
        copy.wait()


def flip(stored):
    _, columns, width = stored.shape
    shape = (-(-columns // 128), width, 128)
    count = len(EARLY)
    return pl.pallas_call(
        flip_kernel,
        out_shape=(
            jax.ShapeDtypeStruct(shape, jnp.bfloat16),
            jax.ShapeDtypeStruct((count, width, 128), jnp.bfloat16),
        ),
        in_specs=[pl.BlockSpec(memory_space=pl.ANY)],
        out_specs=(pl.BlockSpec(memory_space=pl.ANY),) * 2,
        scratch_shapes=[
            pltpu.VMEM((columns, width), jnp.bfloat16),
            pltpu.VMEM(shape, jnp.bfloat16),
            pltpu.VMEM((count, 128, width), jnp.bfloat16),
            pltpu.VMEM((count, width, 128), jnp.bfloat16),
            pltpu.SemaphoreType.DMA((PARTS + shape[0] + 2 * count,)),
        ],
        cost_estimate=hint(10),
        compiler_params=pltpu.CompilerParams(vmem_limit_bytes=FULL_LIMIT),
    )(stored)


def joint(normed_ref, strips_ref, joined_ref):
    columns = joined_ref.shape[1]
    for j in range(0, -(-columns // 128), 2):
        last = min(j + 2, strips_ref.shape[0])
        weight = jnp.concatenate([strips_ref[i] for i in range(j, last)], axis=1)
        stop = min(last * 128, columns)
        joined_ref[:, j * 128 : stop] = jnp.dot(
            normed_ref[...], weight[:, : stop - j * 128], preferred_element_type=jnp.float32
        ).astype(jnp.bfloat16)


def product(left, right, dims):
    return lax.dot_general(left, right, (((dims[0],), (dims[1],)), ((), ())), preferred_element_type=jnp.float32)


def hint(microseconds):
    return pl.CostEstimate(
        flops=int(microseconds * 1e9), bytes_accessed=int(microseconds * 3e6), transcendentals=0
    )


def column_kernel(
    found_ref, got_ref, w_in_ref, strips_ref, early_ref, w_out_ref, out_ref,
    flat_ref, x_ref, normed_ref, joined_ref, keyed_ref,
):
    rows, depth, tokens = found_ref.shape
    per = out_ref.shape[1]
    width = w_in_ref.shape[2]
    for s in range(rows):
        flat_ref[s * depth : (s + 1) * depth] = found_ref[s]
    for r in range(rows):
        normed_ref[r * per : (r + 1) * per] = got_ref[r, :, :width]
    for i in range(0, width, 128):
        x_ref[:, i : i + 128] = jnp.transpose(flat_ref[i : i + 128]).astype(
            jnp.float32
        ) + normed_ref[:, i : i + 128].astype(jnp.float32)
    normalize(x_ref, normed_ref)
    for i, low in enumerate(EARLY):
        weight = jnp.concatenate(
            [jnp.transpose(w_in_ref[0, low - 128 : low]), early_ref[i]], axis=1
        )
        joined_ref[:, low - 128 : low + 128] = product(
            normed_ref[...], weight, (1, 0)
        ).astype(jnp.bfloat16)
    stop = EARLY[-1] + 128
    joined_ref[:, stop:] = product(
        normed_ref[...], w_in_ref[0, stop:], (1, 1)
    ).astype(jnp.bfloat16)
    joined = joined_ref[...]
    key_of = lax.broadcasted_iota(jnp.int32, (tokens, tokens), 0)
    query_of = lax.broadcasted_iota(jnp.int32, (tokens, tokens), 1)
    allowed = (key_of % per == query_of % per) & (key_of <= query_of)
    query, key, value = (
        [joined[:, 3 * HEAD * h + HEAD * i : 3 * HEAD * h + HEAD * (i + 1)] for h in range(HEADS)]
        for i in range(3)
    )
    scores = [product(k, q, (1, 1)) * (1.0 / math.sqrt(HEAD)) for q, k in zip(query, key)]
    scores = [jnp.where(allowed, s, -jnp.inf) for s in scores]
    top = [jnp.max(s, axis=0, keepdims=True) for s in scores]
    lifted = [jnp.exp(s - m) for s, m in zip(scores, top)]
    share = [1.0 / jnp.sum(e, axis=0, keepdims=True) for e in lifted]
    probs = [(e * r).astype(jnp.bfloat16) for e, r in zip(lifted, share)]
    mixed = jnp.concatenate(
        [product(p, v, (0, 0)).astype(jnp.bfloat16) for p, v in zip(probs, value)], axis=1
    )
    for i in range(0, width, OUT_STEP):
        span = slice(i, min(i + OUT_STEP, width))
        x_ref[:, span] += jnp.dot(
            mixed, w_out_ref[0, :, span], preferred_element_type=jnp.float32
        )
    normalize(x_ref, normed_ref)
    joint(normed_ref, strips_ref, keyed_ref)
    resid = x_ref[...].astype(jnp.bfloat16)
    out_ref[0, :, width:] = jnp.zeros((per, keyed_ref.shape[1]), jnp.bfloat16)
    for r in range(rows):
        out_ref[r, :, :width] = resid[r * per : (r + 1) * per]
        if r + 1 < rows:
            out_ref[r + 1, :, width:] = keyed_ref[r * per : (r + 1) * per]


def column_sublayer(found, got, w_in, strips, early, w_out):
    rows, depth, tokens = found.shape
    width = w_in.shape[2]
    per = tokens // rows
    return pl.pallas_call(
        column_kernel,
        out_shape=jax.ShapeDtypeStruct((rows, per, width + 2 * HEADS * HEAD), jnp.bfloat16),
        in_specs=[pl.BlockSpec(memory_space=pltpu.VMEM)] * 6,
        out_specs=pl.BlockSpec(memory_space=pltpu.VMEM),
        scratch_shapes=[
            pltpu.VMEM((width, tokens), jnp.bfloat16),
            pltpu.VMEM((tokens, width), jnp.float32),
            pltpu.VMEM((tokens, width), jnp.bfloat16),
            pltpu.VMEM((tokens, 3 * HEADS * HEAD), jnp.bfloat16),
            pltpu.VMEM((tokens, 2 * HEADS * HEAD), jnp.bfloat16),
        ],
        cost_estimate=hint(20),
        compiler_params=pltpu.CompilerParams(vmem_limit_bytes=VMEM_LIMIT),
    )(found, got, w_in, strips, early, w_out)


def row_kernel(got_ref, strips_ref, w_out_ref, out_ref, x_ref, normed_ref, before_ref, joined_ref):
    rows, per, _ = got_ref.shape
    width = strips_ref.shape[1]
    has_before = lax.axis_index("seq") > 0
    inv_root = 1.0 / math.sqrt(HEAD)
    for r in range(rows):
        normed_ref[r * per : (r + 1) * per] = got_ref[r, :, :width]
        before_ref[r * per : (r + 1) * per] = got_ref[r, :, width:]
    x_ref[...] = normed_ref[...].astype(jnp.float32)
    normalize(x_ref, normed_ref)
    joint(normed_ref, strips_ref, joined_ref)
    joined = joined_ref[...]
    before = before_ref[...]
    tokens = joined.shape[0]
    own = lax.broadcasted_iota(jnp.int32, (tokens, tokens), 0) == lax.broadcasted_iota(
        jnp.int32, (tokens, tokens), 1
    )
    start = 2 * HEADS * HEAD
    query = [joined[:, start + HEAD * h : start + HEAD * (h + 1)] for h in range(HEADS)]
    own_key, far_key, own_value, far_value = (
        [part[:, HEAD * (2 * h + i) : HEAD * (2 * h + i + 1)] for h in range(HEADS)]
        for i in range(2)
        for part in (joined, before)
    )
    far = [product(k, q, (1, 1)) * inv_root for q, k in zip(query, far_key)]
    far = [jnp.where(has_before, s, -jnp.inf) for s in far]
    near = [product(k, q, (1, 1)) * inv_root for q, k in zip(query, own_key)]
    near = [jnp.sum(jnp.where(own, s, 0.0), axis=0, keepdims=True) for s in near]
    top = [jnp.maximum(jnp.max(f, axis=0, keepdims=True), n) for f, n in zip(far, near)]
    far = [jnp.exp(f - m) for f, m in zip(far, top)]
    near = [jnp.exp(n - m) for n, m in zip(near, top)]
    share = [1.0 / (jnp.sum(f, axis=0, keepdims=True) + n) for f, n in zip(far, near)]
    far = [(f * r).astype(jnp.bfloat16) for f, r in zip(far, share)]
    near = [jnp.where(own, n * r, 0.0).astype(jnp.bfloat16) for n, r in zip(near, share)]
    mixed = jnp.concatenate(
        [
            product(
                jnp.concatenate([far[h], near[h]], axis=0),
                jnp.concatenate([far_value[h], own_value[h]], axis=0),
                (0, 0),
            ).astype(jnp.bfloat16)
            for h in range(HEADS)
        ],
        axis=1,
    )
    for i in range(0, width, OUT_STEP):
        span = slice(i, min(i + OUT_STEP, width))
        out_ref[:, span] = (
            x_ref[:, span]
            + jnp.dot(mixed, w_out_ref[1, :, span], preferred_element_type=jnp.float32)
        ).astype(jnp.bfloat16)


def row_sublayer(got, strips, w_out):
    rows, per, _ = got.shape
    tokens = rows * per
    width = strips.shape[1]
    return pl.pallas_call(
        row_kernel,
        out_shape=jax.ShapeDtypeStruct((tokens, width), jnp.bfloat16),
        in_specs=[pl.BlockSpec(memory_space=pltpu.VMEM)] * 3,
        out_specs=pl.BlockSpec(memory_space=pltpu.VMEM),
        scratch_shapes=[
            pltpu.VMEM((tokens, width), jnp.float32),
            pltpu.VMEM((tokens, width), jnp.bfloat16),
            pltpu.VMEM((tokens, 2 * HEADS * HEAD), jnp.bfloat16),
            pltpu.VMEM((tokens, 3 * HEADS * HEAD), jnp.bfloat16),
        ],
        cost_estimate=hint(20),
        compiler_params=pltpu.CompilerParams(vmem_limit_bytes=VMEM_LIMIT),
    )(got, strips, w_out)


def lookup_kernel(got_ref, table_ref, out_ref, turned_ref, codes_ref):
    depth, entries = table_ref.shape
    step = entries // GROUPS
    count = out_ref.shape[0]
    padded = (depth + 7) // 8 * 8
    flipped = jnp.concatenate(
        [table_ref[...].astype(jnp.float32), jnp.zeros((padded - depth, entries), jnp.float32)],
        axis=0,
    )
    stacked = jnp.concatenate(
        [flipped[:, g * step : (g + 1) * step] for g in range(GROUPS)], axis=0
    ).astype(jnp.bfloat16)
    rows, per, total = got_ref.shape
    tokens = rows * per
    for i in range(2):
        digits = got_ref[:, i, total - tokens :].astype(jnp.float32)
        turned_ref[i] = jnp.transpose(
            jnp.concatenate([digits, jnp.zeros((tokens - rows, tokens), jnp.float32)], axis=0)
        )
    row_of = lax.broadcasted_iota(jnp.int32, (tokens, tokens), 0)
    place_of = lax.broadcasted_iota(jnp.int32, (tokens, tokens), 1)
    moved = jnp.zeros((2 * rows, tokens), jnp.float32)
    for c in range(per):
        picked = jnp.concatenate(
            [turned_ref[i, pl.ds(c, rows, stride=per), :] for i in range(2)], axis=0
        ).astype(jnp.bfloat16)
        spread = jnp.where(place_of == per * row_of + c, 1.0, 0.0).astype(jnp.bfloat16)
        moved += jnp.dot(picked, spread, preferred_element_type=jnp.float32)
    codes_ref[...] = moved[:rows].astype(jnp.int32) * DIGIT + moved[rows:].astype(jnp.int32)
    slots = lax.broadcasted_iota(jnp.int32, (step, AT_ONCE * 128), 0)
    slots = slots.astype(jnp.float32).astype(jnp.bfloat16)
    for d in range(0, count, AT_ONCE):
        codes = jnp.concatenate([codes_ref[d + e : d + e + 1, :] for e in range(AT_ONCE)], axis=1)
        low = (codes % step).astype(jnp.float32).astype(jnp.bfloat16)
        high = codes // step
        onehot = jnp.where(slots == low, jnp.bfloat16(1), jnp.bfloat16(0))
        found = jnp.dot(stacked, onehot, preferred_element_type=jnp.float32)
        chosen = jnp.zeros((padded, AT_ONCE * 128), jnp.float32)
        for g in range(GROUPS):
            chosen = jnp.where(high == g, found[g * padded : (g + 1) * padded], chosen)
        for e in range(AT_ONCE):
            out_ref[d + e] = chosen[:depth, e * 128 : (e + 1) * 128].astype(jnp.bfloat16)


def lookup(got, table):
    count = got.shape[0]
    tokens = count * got.shape[1]
    depth = table.shape[0]
    return pl.pallas_call(
        lookup_kernel,
        out_shape=jax.ShapeDtypeStruct((count, depth, 128), jnp.bfloat16),
        in_specs=[pl.BlockSpec(memory_space=pltpu.VMEM)] * 2,
        out_specs=pl.BlockSpec(memory_space=pltpu.VMEM),
        scratch_shapes=[
            pltpu.VMEM((2, tokens, tokens), jnp.float32),
            pltpu.VMEM((count, tokens), jnp.int32),
        ],
        cost_estimate=hint(140),
        compiler_params=pltpu.CompilerParams(vmem_limit_bytes=VMEM_LIMIT),
    )(got, table)


def pack_kernel(codes_hbm, position_hbm, out_hbm, codes_ref, position_ref, out_ref, sem):
    rows, per, _ = out_ref.shape
    tokens, width = position_ref.shape
    part = rows // PARTS
    fetch = [pltpu.make_async_copy(codes_hbm, codes_ref, sem.at[0])]
    for i in range(PARTS):
        span = pl.ds(i * part * per, part * per)
        fetch.append(
            pltpu.make_async_copy(position_hbm.at[span], position_ref.at[span], sem.at[1 + i])
        )
    for copy in fetch:
        copy.start()
    fetch[0].wait()
    codes = codes_ref[...]
    digits = jnp.concatenate([codes // DIGIT, codes % DIGIT], axis=0).astype(jnp.bfloat16)
    store = []
    for i in range(PARTS):
        fetch[1 + i].wait()
        for r in range(i * part, (i + 1) * part):
            out_ref[r, :, :width] = position_ref[r * per : (r + 1) * per]
            out_ref[r, :, width:] = digits
        span = pl.ds(i * part, part)
        store.append(pltpu.make_async_copy(out_ref.at[span], out_hbm.at[span], sem.at[1 + PARTS + i]))
        store[-1].start()
    for copy in store:
        copy.wait()


def pack(song_ids, position_table, rows):
    tokens, width = position_table.shape
    shape = (rows, tokens // rows, width + tokens)
    return pl.pallas_call(
        pack_kernel,
        out_shape=jax.ShapeDtypeStruct(shape, jnp.bfloat16),
        in_specs=[pl.BlockSpec(memory_space=pl.ANY)] * 2,
        out_specs=pl.BlockSpec(memory_space=pl.ANY),
        scratch_shapes=[
            pltpu.VMEM((1, tokens), jnp.int32),
            pltpu.VMEM((tokens, width), jnp.bfloat16),
            pltpu.VMEM(shape, jnp.bfloat16),
            pltpu.SemaphoreType.DMA((1 + 2 * PARTS,)),
        ],
        cost_estimate=hint(60),
        compiler_params=pltpu.CompilerParams(vmem_limit_bytes=FULL_LIMIT),
    )(song_ids.reshape(1, tokens), position_table)


def exchange(value):
    return lax.all_to_all(value, "seq", split_axis=0, concat_axis=0, tiled=True)


def shards(song_ids, table, position_table, w_qkv, w_out):
    rows = lax.axis_size("seq")
    tokens, width = position_table.shape
    per = tokens // rows

    got = exchange(pack(song_ids, position_table, rows))
    w_in = jnp.swapaxes(w_qkv, 1, 2)
    strips, early = flip(w_in)
    got, strips, early = lax.optimization_barrier((got, strips, early))
    found = exchange(lookup(got, jnp.transpose(table)))
    got = exchange(column_sublayer(found, got, w_in, strips, early, w_out))
    return row_sublayer(got, strips, w_out)


def solution(mesh):
    in_specs = (P(("song", "seq")), P(None, "seq"), P("seq", None), P(), P())
    out_specs = P(("song", "seq"), None)
    return jax.shard_map(shards, mesh=mesh, in_specs=in_specs, out_specs=out_specs, check_vma=False)
```
